32 devices in a mesh: energy: 8 (over z, core), slab: 4 (over y, x).
Axes of the slice: x: 2, y: 2, z: 4, core: 2. Of those that a mesh axis runs over, the one named last changes fastest.
Arguments:
- h_diag: float32 [4, 128, 128], P('slab'), may hold values from -0.625 to 0.625, as said below
- coupling: float32 [4, 128, 128], P('slab'), may hold values from -1 to 1
- broadening: float32 [8], P('energy'), may hold values from 0.4 to 1.2
Outputs:
- green: float32 [8, 4, 2, 128, 128], P('energy', 'slab')
- polar: float32 [8, 4, 2, 128, 128], P('energy', 'slab')
The draws below stay inside these ranges and needn't reach their ends.
Inputs may be any that keep to these rules, and one draw needn't show every extreme that they name: h_diag[i] is symmetric for every slab i.
All inputs are finite; a program needn't handle non-finite values.
Results may differ from the reference program's by a relative error of at most 0.0003.
Values sent between devices are 32-bit elements; how exact they have to be, the bound alone decides.
No kernel may reach another device: no remote copies, remote signals or barrier semaphores. Data moves between devices by JAX's collectives and lax.ppermute only.
A program may use at most 64 MiB of HBM per device.

```python
import math
import jax
import jax.numpy as jnp
from jax import lax

B = 128
NE = 8
NS = 4


def draw_h_diag(key, part):
    entries = jnp.clip(jax.random.normal(key, (NS, B, B), jnp.float32), -5.0, 5.0)
    return (entries + jnp.swapaxes(entries, 1, 2)) / jnp.sqrt(2.0 * B)


def steps_of(stream_key, dims, shards, low, top_value):
    level, own = 1.0, jax.random.fold_in(stream_key, 6)
    for dim, shards_of in shards:
        steps = jnp.exp(jax.random.uniform(jax.random.fold_in(own, dim), (shards_of,), jnp.float32, low / len(shards), top_value / len(shards)))
        level = level * jnp.repeat(steps, dims[dim] // shards_of).reshape([-1 if axis == dim else 1 for axis in range(len(dims))])
    return level


def normal_values(key, extent, width, bound, cuts=(), kind=jnp.bfloat16):
    gain = steps_of(key, extent, cuts, -0.22, 0.18) if cuts else 1.0
    array = jax.random.normal(key, extent, jnp.float32) * width * gain
    return jnp.minimum(jnp.maximum(array, -bound), bound).astype(kind)


def setup_inputs(seed: int = 0) -> dict:
    arg_keys = jax.random.split(jax.random.key(seed), 4)
    return {
        "h_diag": draw_h_diag(jax.random.fold_in(arg_keys[3], 71), 0),
        "coupling": normal_values(arg_keys[1], (NS, B, B), (B // 4) ** -0.5, 1.0, ((0, 4),), jnp.float32),
        "broadening": jnp.clip(jnp.exp(math.log(1.2) - 1.0986123 * jax.random.uniform(arg_keys[2], (NE,), jnp.float32) ** steps_of(arg_keys[2], (NE,), ((0, 8),), -0.2, 0.2)), 0.4, 1.2),
    }


highest = lax.Precision.HIGHEST

def matrix_product(left, right):
    return jnp.dot(left.astype(jnp.float32), right.astype(jnp.float32), precision=highest, preferred_element_type=jnp.float32)

def sandwich(left, pair, right):
    return jnp.stack([matrix_product(matrix_product(left, pair[0]), right), matrix_product(matrix_product(left, pair[1]), right)])

def complex_inverse(pair):
    size = pair.shape[-1]
    upper = jnp.concatenate([pair[0], -pair[1]], axis=1)
    lower = jnp.concatenate([pair[1], pair[0]], axis=1)
    real_form = jnp.concatenate([upper, lower], axis=0)
    basis = jnp.concatenate([jnp.eye(size, dtype=jnp.float32), jnp.zeros((size, size), jnp.float32)], axis=0)
    solved = jnp.linalg.solve(real_form, basis)
    return jnp.stack([solved[:size], solved[size:]])

def chain_green(energy, damping, h_diag, coupling):
    slabs = h_diag.shape[0]
    size = h_diag.shape[-1]
    identity = jnp.eye(size, dtype=jnp.float32)
    last_link = coupling[slabs - 1]
    lead = 0.5 * matrix_product(last_link, last_link.T)
    diagonals = []
    for slab in range(slabs):
        imag_part = damping * identity
        if slab == slabs - 1:
            imag_part = imag_part + lead
        diagonals.append(jnp.stack([energy * identity - h_diag[slab], imag_part]))
    zero_pair = jnp.zeros((2, size, size), jnp.float32)
    from_left = [zero_pair]
    for slab in range(1, slabs):
        surface = complex_inverse(diagonals[slab - 1] - from_left[slab - 1])
        from_left.append(sandwich(coupling[slab - 1].T, surface, coupling[slab - 1]))
    from_right = [zero_pair] * slabs
    for slab in range(slabs - 2, -1, -1):
        surface = complex_inverse(diagonals[slab + 1] - from_right[slab + 1])
        from_right[slab] = sandwich(coupling[slab], surface, coupling[slab].T)
    return jnp.stack([complex_inverse(diagonals[slab] - from_left[slab] - from_right[slab]) for slab in range(slabs)])

def reference(h_diag, coupling, broadening):
    count = broadening.shape[0]
    energies = -4.0 + 8.0 * jnp.arange(count, dtype=jnp.float32) / (count - 1)
    green = lax.map(lambda item: chain_green(item[0], item[1], h_diag, coupling), (energies, broadening))
    pieces = []
    for offset in range(count):
        later = green[offset:]
        earlier = green[:count - offset]
        real_part = jnp.sum(later[:, :, 0] * earlier[:, :, 0] + later[:, :, 1] * earlier[:, :, 1], axis=0)
        imag_part = jnp.sum(later[:, :, 1] * earlier[:, :, 0] - later[:, :, 0] * earlier[:, :, 1], axis=0)
        pieces.append(jnp.stack([real_part, imag_part], axis=1) / count)
    polar = jnp.stack(pieces)
    return (green, polar)
```

```python
import functools

import jax
import jax.numpy as jnp
from jax import lax
from jax.experimental import pallas as pl
from jax.experimental.pallas import tpu as pltpu
from jax.sharding import PartitionSpec as P

f32 = jnp.float32
bf16 = jnp.bfloat16
highest = lax.Precision.HIGHEST
PANEL = 32
TILE = 8


def dot(left, right, dims=((1,), (0,))):
    return lax.dot_general(left, right, (dims, ((), ())), precision=highest, preferred_element_type=f32)


def three_parts(value):
    high = value.astype(bf16)
    rest = value - high.astype(f32)
    middle = rest.astype(bf16)
    low = (rest - middle.astype(f32)).astype(bf16)
    return high, middle, low


def row_of(tile, k):
    return jnp.broadcast_to(tile[k : k + 1, :], tile.shape)


def column_of(tile, k):
    return jnp.broadcast_to(tile[:, k : k + 1], tile.shape)


def eliminate_tile(real, imag, base, row, lane):
    height = real.shape[0]
    dr = [column_of(real, base + k) for k in range(height)]
    di = [column_of(imag, base + k) for k in range(height)]
    for k in range(height):
        at_row = row == k
        pr, pi = row_of(dr[k], k), row_of(di[k], k)
        inverse = 1.0 / (pr * pr + pi * pi)
        cr, ci = jnp.where(at_row, -1.0, dr[k]), jnp.where(at_row, 0.0, di[k])
        tr, ti = cr * pr + ci * pi, ci * pr - cr * pi
        fr, fi = tr * inverse, ti * inverse
        for c in range(k + 1, height):
            ar, ai = row_of(dr[c], k), row_of(di[c], k)
            zr, zi = jnp.where(at_row, 0.0, dr[c]), jnp.where(at_row, 0.0, di[c])
            if c == k + 1:
                dr[c] = zr - (tr * ar - ti * ai) * inverse
                di[c] = zi - (tr * ai + ti * ar) * inverse
            else:
                dr[c], di[c] = zr - (fr * ar - fi * ai), zi - (fr * ai + fi * ar)
        at_lane = lane == base + k
        ar = jnp.where(at_lane, 1.0, row_of(real, k))
        ai = jnp.where(at_lane, 0.0, row_of(imag, k))
        cleared = at_row | at_lane
        real = jnp.where(cleared, 0.0, real) - (fr * ar - fi * ai)
        imag = jnp.where(cleared, 0.0, imag) - (fr * ai + fi * ar)
    return real, imag


def eliminate_panel(real, imag, row, lane):
    tiles = len(real)
    for s in range(tiles):
        base = s * TILE
        columns = {
            t: [(column_of(real[t], base + k), column_of(imag[t], base + k)) for k in range(TILE)]
            for t in range(tiles)
            if t != s
        }
        new_real, new_imag = eliminate_tile(real[s], imag[s], base, row, lane)
        rows = [(row_of(new_real, k), row_of(new_imag, k)) for k in range(TILE)]
        inside = (lane >= base) & (lane < base + TILE)
        for t in [(s + 1 + u) % tiles for u in range(tiles - 1)]:
            xr, xi = jnp.where(inside, 0.0, real[t]), jnp.where(inside, 0.0, imag[t])
            for (cr, ci), (wr, wi) in zip(columns[t], rows):
                xr, xi = xr - (cr * wr - ci * wi), xi - (cr * wi + ci * wr)
            real[t], imag[t] = xr, xi
        real[s], imag[s] = new_real, new_imag
    return real, imag


def swept(ref, m):
    size = ref.shape[-1]
    width = min(PANEL, size)
    tiles = width // TILE
    row = lax.broadcasted_iota(jnp.int32, (TILE, size), 0)
    lane = lax.broadcasted_iota(jnp.int32, (TILE, size), 1)
    real = [ref[m, 0, t * TILE : (t + 1) * TILE, :] for t in range(tiles)]
    imag = [ref[m, 1, t * TILE : (t + 1) * TILE, :] for t in range(tiles)]
    lh, lm, ll = three_parts(jnp.concatenate(real + imag, 0))
    real, imag = eliminate_panel(real, imag, row, lane)
    block = lane < width
    wr = jnp.concatenate([pltpu.roll(jnp.where(block, -x, x), size - width, 1) for x in real], 0)
    wi = jnp.concatenate([pltpu.roll(jnp.where(block, -x, x), size - width, 1) for x in imag], 0)
    rh, rm, rl = three_parts(
        jnp.concatenate([jnp.concatenate([wr, wi], 1), jnp.concatenate([-wi, wr], 1)], 0)
    )
    change = lax.dot_general(
        jnp.concatenate([lh, lh, lm, lh, lm, ll], 0),
        jnp.concatenate([rh, rm, rh, rl, rm, rh], 0),
        (((0,), (0,)), ((), ())),
        preferred_element_type=f32,
    )
    cleared = lax.broadcasted_iota(jnp.int32, (size - width, size), 1) < width
    rest_real = pltpu.roll(jnp.where(cleared, 0.0, ref[m, 0, width:, :]), size - width, 1)
    rest_imag = pltpu.roll(jnp.where(cleared, 0.0, ref[m, 1, width:, :]), size - width, 1)
    return rest_real - change[width:, :size], rest_imag - change[width:, size:], wr, wi


def invert_in_place(ref, count):
    size = ref.shape[-1]
    width = min(PANEL, size)

    def step(_, carry):
        results = [swept(ref, m) for m in range(count)]
        for m, (rest_real, rest_imag, wr, wi) in enumerate(results):
            ref[m, 0, : size - width, :] = rest_real
            ref[m, 1, : size - width, :] = rest_imag
            ref[m, 0, size - width :, :] = wr
            ref[m, 1, size - width :, :] = wi
        return carry

    lax.fori_loop(0, size // width, step, 0)


def wide(real, imag):
    return jnp.concatenate([real, imag], 1)


def square(real, imag):
    return jnp.concatenate([wide(real, imag), wide(-imag, real)], 0)


def chain_kernel(count, total_energies, place_ref, damping_ref, *refs):
    blocks, (green_ref, diagonal_ref, link_ref, work_ref) = refs[: 2 * count], refs[2 * count :]
    h_refs, c_refs = blocks[:count], blocks[count:]
    size = green_ref.shape[-1]
    slab, position = place_ref[0], place_ref[1]
    energy = -4.0 + 8.0 * position.astype(f32) / (total_energies - 1)
    damping = damping_ref[0]
    row = lax.broadcasted_iota(jnp.int32, (size, size), 0)
    lane = lax.broadcasted_iota(jnp.int32, (size, size), 1)
    identity = jnp.where(row == lane, 1.0, 0.0).astype(f32)

    def is_last(step):
        return lax.rem(slab + step, count) == count - 1

    def cut_link(step):
        return c_refs[step][...] * jnp.where(is_last(step), 0.0, 1.0)

    for step in range(count):
        diagonal_ref[step, 0] = energy * identity - h_refs[step][...]
        diagonal_ref[step, 1] = damping * identity

        @pl.when(is_last(step))
        def _():
            link = c_refs[step][...]
            diagonal_ref[step, 1] = diagonal_ref[step, 1] + 0.5 * dot(link, link, ((1,), (1,)))

    def subtract(node, real, imag):
        diagonal_ref[node, 0] = diagonal_ref[node, 0] - real
        diagonal_ref[node, 1] = diagonal_ref[node, 1] - imag

    for level in range(count.bit_length() - 1):
        stride = 1 << level
        nodes = list(range(0, count, stride))
        odds = nodes[1::2]
        for first in range(0, len(odds), 2):
            group = odds[first : first + 2]
            for m, node in enumerate(group):
                work_ref[m] = diagonal_ref[node]
            invert_in_place(work_ref, len(group))
            for m, node in enumerate(group):
                before, after = node - stride, (node + stride) % count
                middle = (work_ref[m, 0], work_ref[m, 1])
                if level == 0:
                    left = (cut_link(before), None)
                    right = (cut_link(node).T, None)
                else:
                    left = (link_ref[before, 0], link_ref[before, 1])
                    right = (link_ref[node, 0].T, link_ref[node, 1].T)
                if before == after:
                    left = tuple(None if a is None else a + b for a, b in zip(left, right))

                def reached(pair):
                    if pair[1] is None:
                        both = dot(pair[0], wide(*middle))
                    else:
                        both = dot(wide(*pair), square(*middle))
                    return both[:, :size], both[:, size:]

                def closed(pair, end):
                    if end[1] is None:
                        both = dot(jnp.concatenate(pair, 0), end[0], ((1,), (1,)))
                        return both[:size], both[size:]
                    turned = jnp.concatenate([wide(end[0], -end[1]), wide(end[1], end[0])], 0)
                    both = dot(wide(*pair), turned, ((1,), (1,)))
                    return both[:, :size], both[:, size:]

                start = reached(left)
                real, imag = closed(start, left)
                subtract(before, -real, -imag)
                if before != after:
                    real, imag = closed(start, right)
                    link_ref[before, 0] = real
                    link_ref[before, 1] = imag
                    real, imag = closed(reached(right), right)
                    subtract(after, -real, -imag)
    work_ref[0] = diagonal_ref[0]
    invert_in_place(work_ref, 1)
    green_ref[...] = -work_ref[0]


def green_of(h_blocks, c_blocks, slab, position, damping, total_energies):
    count, size = len(h_blocks), h_blocks[0].shape[-1]
    whole = pl.BlockSpec(memory_space=pltpu.VMEM)
    scalar = pl.BlockSpec(memory_space=pltpu.SMEM)
    return pl.pallas_call(
        functools.partial(chain_kernel, count, total_energies),
        out_shape=jax.ShapeDtypeStruct((2, size, size), f32),
        in_specs=[scalar, scalar] + [whole] * (2 * count),
        out_specs=whole,
        scratch_shapes=[
            pltpu.VMEM((count, 2, size, size), f32),
            pltpu.VMEM((count, 2, size, size), f32),
            pltpu.VMEM((2, 2, size, size), f32),
        ],
        name="chain",
    )(jnp.stack([slab, position]).astype(jnp.int32), damping, *h_blocks, *c_blocks)


def correlate(own, groups):
    gathered = [own] + [
        lax.ppermute(own, "energy", [(s, s ^ d) for s in range(groups)]) for d in range(2, groups, 2)
    ]
    everything = []
    for block in gathered:
        everything.append(block)
        everything.append(lax.ppermute(block, "energy", [(s, s ^ 1) for s in range(groups)]))
    mine = lax.axis_index("energy")

    def kernel(mine_ref, *refs):
        blocks, (out_ref, held) = refs[:groups], refs[groups:]
        me = mine_ref[0]
        for step in range(groups):
            held[me ^ step] = blocks[step][...]
        real = imag = jnp.zeros(own.shape[1:], f32)
        for first in range(groups):
            inside = first + me < groups
            second = jnp.where(inside, first + me, 0)
            weight = jnp.where(inside, 1.0 / groups, 0.0)
            br, bi = held[first, 0] * weight, held[first, 1] * weight
            ar, ai = held[second, 0], held[second, 1]
            real = real + (ar * br + ai * bi)
            imag = imag + (ai * br - ar * bi)
        out_ref[0] = real
        out_ref[1] = imag

    whole = pl.BlockSpec(memory_space=pltpu.VMEM)
    return pl.pallas_call(
        kernel,
        out_shape=jax.ShapeDtypeStruct(own.shape, f32),
        in_specs=[pl.BlockSpec(memory_space=pltpu.SMEM)] + [whole] * groups,
        out_specs=whole,
        scratch_shapes=[pltpu.VMEM((groups,) + own.shape, f32)],
        name="polar",
    )(mine[None].astype(jnp.int32), *everything)


def correlate_spread(own, groups):
    _, size, _ = own.shape
    spread = own.reshape(2, groups, size * size // groups)
    mixed = lax.all_to_all(spread[None], "energy", split_axis=2, concat_axis=0, tiled=True)[:, :, 0]
    real, imag = mixed[:, 0], mixed[:, 1]
    pieces = []
    for offset in range(groups):
        ar, ai = real[offset:], imag[offset:]
        br, bi = real[: groups - offset], imag[: groups - offset]
        pieces.append(jnp.stack([jnp.sum(ar * br + ai * bi, 0), jnp.sum(ai * br - ar * bi, 0)]))
    result = (jnp.stack(pieces) / groups)[:, :, None, :]
    back = lax.all_to_all(result, "energy", split_axis=0, concat_axis=2, tiled=True)
    return back.reshape(own.shape)


def on_device(h_diag, coupling, broadening):
    slabs = lax.axis_size("slab")
    groups = lax.axis_size("energy")
    slab = lax.axis_index("slab")
    position = lax.axis_index("energy")
    size = h_diag.shape[-1]
    own = jnp.concatenate([h_diag, coupling], 0)
    blocks = [own] + [
        lax.ppermute(own, "slab", [(s, (s - r) % slabs) for s in range(slabs)]) for r in range(1, slabs)
    ]
    green = green_of([b[0] for b in blocks], [b[1] for b in blocks], slab, position, broadening, groups)
    polar = correlate(green, groups) if groups <= 8 else correlate_spread(green, groups)
    shape = (1, 1, 2, size, size)
    return green.reshape(shape), polar.reshape(shape)


def solution(mesh):
    return jax.shard_map(
        on_device,
        mesh=mesh,
        in_specs=(P("slab", None, None), P("slab", None, None), P("energy")),
        out_specs=(P("energy", "slab", None, None, None), P("energy", "slab", None, None, None)),
        check_vma=False,
    )
```

```python
import functools

import jax
import jax.numpy as jnp
from jax import lax
from jax.experimental import pallas as pl
from jax.experimental.pallas import tpu as pltpu
from jax.sharding import PartitionSpec as P

f32 = jnp.float32
bf16 = jnp.bfloat16
highest = lax.Precision.HIGHEST
PANEL = 16
TILE = 8


def dot(left, right, dims=((1,), (0,))):
    return lax.dot_general(left, right, (dims, ((), ())), precision=highest, preferred_element_type=f32)


def three_parts(value):
    high = value.astype(bf16)
    rest = value - high.astype(f32)
    middle = rest.astype(bf16)
    low = (rest - middle.astype(f32)).astype(bf16)
    return high, middle, low


def row_of(tile, k):
    return jnp.broadcast_to(tile[k : k + 1, :], tile.shape)


def column_of(tile, k):
    return jnp.broadcast_to(tile[:, k : k + 1], tile.shape)


def lanes_at(tile, index):
    return jnp.take_along_axis(tile, index, axis=1, mode="promise_in_bounds")


def spread_columns(real, imag, base):
    index = [jnp.zeros(real.shape, jnp.int32) + (base + k) for k in range(TILE)]
    return [lanes_at(real, i) for i in index], [lanes_at(imag, i) for i in index]


def eliminate_tiles(pairs, base, row, lane):
    columns = [spread_columns(real, imag, base) for real, imag in pairs]
    pairs = list(pairs)
    for k in range(TILE):
        at_row = row == k
        at_lane = lane == base + k
        cleared = at_row | at_lane
        factors = []
        for dr, di in columns:
            pr, pi = row_of(dr[k], k), row_of(di[k], k)
            inverse = 1.0 / (pr * pr + pi * pi)
            cr, ci = jnp.where(at_row, -1.0, dr[k]), jnp.where(at_row, 0.0, di[k])
            tr, ti = cr * pr + ci * pi, ci * pr - cr * pi
            factors.append((tr, ti, inverse, tr * inverse, ti * inverse))
        for c in range(k + 1, TILE):
            for (dr, di), (tr, ti, inverse, fr, fi) in zip(columns, factors):
                ar, ai = row_of(dr[c], k), row_of(di[c], k)
                zr, zi = jnp.where(at_row, 0.0, dr[c]), jnp.where(at_row, 0.0, di[c])
                if c == k + 1:
                    dr[c] = zr - (tr * ar - ti * ai) * inverse
                    di[c] = zi - (tr * ai + ti * ar) * inverse
                else:
                    dr[c], di[c] = zr - (fr * ar - fi * ai), zi - (fr * ai + fi * ar)
        for m, ((real, imag), (_, _, _, fr, fi)) in enumerate(zip(pairs, factors)):
            ar = jnp.where(at_lane, 1.0, row_of(real, k))
            ai = jnp.where(at_lane, 0.0, row_of(imag, k))
            pairs[m] = (
                jnp.where(cleared, 0.0, real) - (fr * ar - fi * ai),
                jnp.where(cleared, 0.0, imag) - (fr * ai + fi * ar),
            )
    return pairs


def eliminate_panel(panels, first, row, lane):
    tiles = len(panels[0])
    for s in range(tiles):
        base = first + s * TILE
        others = [(s + 1 + u) % tiles for u in range(tiles - 1)]
        columns = [{t: spread_columns(*panel[t], base) for t in others} for panel in panels]
        done = eliminate_tiles([panel[s] for panel in panels], base, row, lane)
        rows = [[(row_of(real, k), row_of(imag, k)) for k in range(TILE)] for real, imag in done]
        inside = (lane >= base) & (lane < base + TILE)
        for t in others:
            for m, panel in enumerate(panels):
                real, imag = panel[t]
                real, imag = jnp.where(inside, 0.0, real), jnp.where(inside, 0.0, imag)
                for cr, ci, (wr, wi) in zip(*columns[m][t], rows[m]):
                    real, imag = real - (cr * wr - ci * wi), imag - (cr * wi + ci * wr)
                panel[t] = (real, imag)
        for m, panel in enumerate(panels):
            panel[s] = done[m]
    return panels


def invert_in_place(ref, count):
    size = ref.shape[-1]
    width = min(PANEL, size)
    tiles = width // TILE

    def step(j, carry):
        first = j * width
        row = lax.broadcasted_iota(jnp.int32, (TILE, size), 0)
        lane = lax.broadcasted_iota(jnp.int32, (TILE, size), 1)
        panels, lefts, results = [], [], []
        for m in range(count):
            at = [pl.ds(pl.multiple_of(first + t * TILE, TILE), TILE) for t in range(tiles)]
            panels.append([(ref[m, 0, rows, :], ref[m, 1, rows, :]) for rows in at])
            parts = [real for real, _ in panels[m]] + [imag for _, imag in panels[m]]
            lh, lm, ll = three_parts(jnp.concatenate(parts, 0))
            lefts.append(jnp.concatenate([lh, lh, lm, lh, lm, ll], 0))
        panels = eliminate_panel(panels, first, row, lane)
        block = (lane >= first) & (lane < first + width)
        full_lane = lax.broadcasted_iota(jnp.int32, (size, size), 1)
        cleared = (full_lane >= first) & (full_lane < first + width)
        for m in range(count):
            wr = jnp.concatenate([jnp.where(block, -real, real) for real, _ in panels[m]], 0)
            wi = jnp.concatenate([jnp.where(block, -imag, imag) for _, imag in panels[m]], 0)
            rh, rm, rl = three_parts(square(wr, wi))
            change = lax.dot_general(
                lefts[m],
                jnp.concatenate([rh, rm, rh, rl, rm, rh], 0),
                (((0,), (0,)), ((), ())),
                preferred_element_type=f32,
            )
            real = jnp.where(cleared, 0.0, ref[m, 0]) - change[:, :size]
            imag = jnp.where(cleared, 0.0, ref[m, 1]) - change[:, size:]
            results.append((real, imag, wr, wi))
        for m, (real, imag, wr, wi) in enumerate(results):
            rows = pl.ds(pl.multiple_of(first, width), width)
            ref[m, 0] = real
            ref[m, 1] = imag
            ref[m, 0, rows, :] = wr
            ref[m, 1, rows, :] = wi
        return carry

    lax.fori_loop(0, size // width, step, 0)


def wide(real, imag):
    return jnp.concatenate([real, imag], 1)


def square(real, imag):
    return jnp.concatenate([wide(real, imag), wide(-imag, real)], 0)


def packed_half(value):
    size = value.shape[0]
    half = size // 2
    row = lax.broadcasted_iota(jnp.int32, (half, size), 0)
    lane = lax.broadcasted_iota(jnp.int32, (half, size), 1)
    quarters = jnp.where((lane < half) | (lane - half > row), pltpu.roll(value[:half], half, 1), value[half:])
    full_row = lax.broadcasted_iota(jnp.int32, (size, size), 0)
    full_lane = lax.broadcasted_iota(jnp.int32, (size, size), 1)
    diagonal = jnp.sum(jnp.where(full_row == full_lane, value, 0.0), axis=0, keepdims=True)
    return jnp.concatenate([quarters, jnp.broadcast_to(diagonal, (TILE, size))], 0)


def unpacked(packed):
    size = packed.shape[1]
    half = size // 2
    quarters = packed[:half]
    whole = jnp.concatenate([pltpu.roll(quarters, half, 1), quarters], 0)
    row = lax.broadcasted_iota(jnp.int32, (size, size), 0)
    lane = lax.broadcasted_iota(jnp.int32, (size, size), 1)
    as_is = ((row < half) & (lane > row)) | ((row >= half) & (lane >= half) & (lane < row))
    full = jnp.where(as_is, whole, whole.T)
    return jnp.where(row == lane, jnp.broadcast_to(packed[half : half + 1], (size, size)), full)


def chain_kernel(count, total_energies, damping_ref, *refs):
    blocks, (green_ref, packed_ref, diagonal_ref, link_ref, work_ref) = refs[:count], refs[count:]
    h_refs, c_refs = [block.at[0] for block in blocks], [block.at[1] for block in blocks]
    size = green_ref.shape[-1]
    slab, position = lax.axis_index("slab"), lax.axis_index("energy")
    energy = -4.0 + 8.0 * position.astype(f32) / (total_energies - 1)
    damping = damping_ref[0]
    row = lax.broadcasted_iota(jnp.int32, (size, size), 0)
    lane = lax.broadcasted_iota(jnp.int32, (size, size), 1)
    identity = jnp.where(row == lane, 1.0, 0.0).astype(f32)

    def is_last(step):
        return lax.rem(slab + step, count) == count - 1

    def cut_link(step):
        return c_refs[step][...] * jnp.where(is_last(step), 0.0, 1.0)

    for step in range(count):
        diagonal_ref[step, 0] = energy * identity - h_refs[step][...]
        diagonal_ref[step, 1] = damping * identity

        @pl.when(is_last(step))
        def _():
            link = c_refs[step][...]
            diagonal_ref[step, 1] = diagonal_ref[step, 1] + 0.5 * dot(link, link, ((1,), (1,)))

    def subtract(node, real, imag):
        diagonal_ref[node, 0] = diagonal_ref[node, 0] - real
        diagonal_ref[node, 1] = diagonal_ref[node, 1] - imag

    for level in range(count.bit_length() - 1):
        stride = 1 << level
        nodes = list(range(0, count, stride))
        odds = nodes[1::2]
        for first in range(0, len(odds), 2):
            group = odds[first : first + 2]
            for m, node in enumerate(group):
                work_ref[m] = diagonal_ref[node]
            invert_in_place(work_ref, len(group))
            for m, node in enumerate(group):
                before, after = node - stride, (node + stride) % count
                middle = (work_ref[m, 0], work_ref[m, 1])
                if level == 0:
                    left = (cut_link(before), None)
                    right = (cut_link(node).T, None)
                else:
                    left = (link_ref[before, 0], link_ref[before, 1])
                    right = (link_ref[node, 0].T, link_ref[node, 1].T)
                if before == after:
                    left = tuple(None if a is None else a + b for a, b in zip(left, right))

                def reached(pair):
                    if pair[1] is None:
                        both = dot(pair[0], wide(*middle))
                    else:
                        both = dot(wide(*pair), square(*middle))
                    return both[:, :size], both[:, size:]

                def closed(pair, end):
                    if end[1] is None:
                        both = dot(jnp.concatenate(pair, 0), end[0], ((1,), (1,)))
                        return both[:size], both[size:]
                    turned = jnp.concatenate([wide(end[0], -end[1]), wide(end[1], end[0])], 0)
                    both = dot(wide(*pair), turned, ((1,), (1,)))
                    return both[:, :size], both[:, size:]

                start = reached(left)
                real, imag = closed(start, left)
                subtract(before, -real, -imag)
                if before != after:
                    real, imag = closed(start, right)
                    link_ref[before, 0] = real
                    link_ref[before, 1] = imag
                    real, imag = closed(reached(right), right)
                    subtract(after, -real, -imag)
    work_ref[0] = diagonal_ref[0]
    invert_in_place(work_ref, 1)
    for part in range(2):
        value = -work_ref[0, part]
        green_ref[part] = value
        packed_ref[part] = packed_half(value)


def green_of(blocks, damping, total_energies):
    count, size = len(blocks), blocks[0].shape[-1]
    whole = pl.BlockSpec(memory_space=pltpu.VMEM)
    scalar = pl.BlockSpec(memory_space=pltpu.SMEM)
    return pl.pallas_call(
        functools.partial(chain_kernel, count, total_energies),
        out_shape=(
            jax.ShapeDtypeStruct((2, size, size), f32),
            jax.ShapeDtypeStruct((2, size // 2 + TILE, size), f32),
        ),
        in_specs=[scalar] + [whole] * count,
        out_specs=(whole, whole),
        scratch_shapes=[
            pltpu.VMEM((count, 2, size, size), f32),
            pltpu.VMEM((count, 2, size, size), f32),
            pltpu.VMEM((2, 2, size, size), f32),
        ],
        name="chain",
    )(damping, *blocks)


def polar_kernel(steps, *refs):
    groups = len(steps)
    blocks, (out_ref, held) = refs[:groups], refs[groups:]
    me = lax.axis_index("energy")
    for step, block in zip(steps, blocks):
        held[me ^ step] = block[...]
    real = imag = jnp.zeros(held.shape[2:], f32)
    for first in range(groups):
        inside = first + me < groups
        second = jnp.where(inside, first + me, 0)
        weight = jnp.where(inside, 1.0 / groups, 0.0)
        br, bi = held[first, 0] * weight, held[first, 1] * weight
        ar, ai = held[second, 0], held[second, 1]
        real = real + (ar * br + ai * bi)
        imag = imag + (ai * br - ar * bi)
    out_ref[0] = unpacked(real)
    out_ref[1] = unpacked(imag)


def correlate(packed, groups):
    def swapped(block, step):
        return lax.ppermute(block, "energy", [(s, s ^ step) for s in range(groups)])

    gathered = [(step, swapped(packed, step)) for step in range(groups - 2, 0, -2)]
    gathered.insert(0, (0, packed))
    gathered = gathered + [(step ^ 1, swapped(block, 1)) for step, block in gathered]
    steps, blocks = zip(*gathered)
    size = packed.shape[-1]
    whole = pl.BlockSpec(memory_space=pltpu.VMEM)
    return pl.pallas_call(
        functools.partial(polar_kernel, steps),
        out_shape=jax.ShapeDtypeStruct((2, size, size), f32),
        in_specs=[whole] * groups,
        out_specs=whole,
        scratch_shapes=[pltpu.VMEM((groups,) + packed.shape, f32)],
        name="polar",
    )(*blocks)


def correlate_spread(own, groups):
    _, size, _ = own.shape
    spread = own.reshape(2, groups, size * size // groups)
    mixed = lax.all_to_all(spread[None], "energy", split_axis=2, concat_axis=0, tiled=True)[:, :, 0]
    real, imag = mixed[:, 0], mixed[:, 1]
    pieces = []
    for offset in range(groups):
        ar, ai = real[offset:], imag[offset:]
        br, bi = real[: groups - offset], imag[: groups - offset]
        pieces.append(jnp.stack([jnp.sum(ar * br + ai * bi, 0), jnp.sum(ai * br - ar * bi, 0)]))
    result = (jnp.stack(pieces) / groups)[:, :, None, :]
    back = lax.all_to_all(result, "energy", split_axis=0, concat_axis=2, tiled=True)
    return back.reshape(own.shape)


def on_device(h_diag, coupling, broadening):
    slabs = lax.axis_size("slab")
    groups = lax.axis_size("energy")
    size = h_diag.shape[-1]
    own = jnp.concatenate([h_diag, coupling], 0)
    blocks = [own] + [
        lax.ppermute(own, "slab", [(s, (s - r) % slabs) for s in range(slabs)]) for r in range(1, slabs)
    ]
    green, packed = green_of(blocks, broadening, groups)
    polar = correlate(packed, groups) if groups <= 8 else correlate_spread(green, groups)
    shape = (1, 1, 2, size, size)
    return green.reshape(shape), polar.reshape(shape)


def solution(mesh):
    return jax.shard_map(
        on_device,
        mesh=mesh,
        in_specs=(P("slab", None, None), P("slab", None, None), P("energy")),
        out_specs=(P("energy", "slab", None, None, None), P("energy", "slab", None, None, None)),
        check_vma=False,
    )
```

```python
import functools

import jax
import jax.numpy as jnp
from jax import lax
from jax.experimental import pallas as pl
from jax.experimental.pallas import tpu as pltpu
from jax.sharding import PartitionSpec as P

f32 = jnp.float32
bf16 = jnp.bfloat16
PANEL = 16
TILE = 8


def three_parts(value):
    high = value.astype(bf16)
    rest = value - high.astype(f32)
    middle = rest.astype(bf16)
    low = (rest - middle.astype(f32)).astype(bf16)
    return high, middle, low


def row_of(tile, k):
    return jnp.broadcast_to(tile[k : k + 1, :], tile.shape)


def column_of(tile, k):
    return jnp.broadcast_to(tile[:, k : k + 1], tile.shape)


def lanes_at(tile, index):
    return jnp.take_along_axis(tile, index, axis=1, mode="promise_in_bounds")


def spread_columns(real, imag, base):
    index = [jnp.zeros(real.shape, jnp.int32) + (base + k) for k in range(TILE)]
    return [lanes_at(real, i) for i in index], [lanes_at(imag, i) for i in index]


def eliminate_tiles(pairs, base, row, lane):
    columns = [spread_columns(real, imag, base) for real, imag in pairs]
    pairs = list(pairs)
    for k in range(TILE):
        at_row = row == k
        at_lane = lane == base + k
        cleared = at_row | at_lane
        factors = []
        for dr, di in columns:
            pr, pi = row_of(dr[k], k), row_of(di[k], k)
            inverse = 1.0 / (pr * pr + pi * pi)
            cr, ci = jnp.where(at_row, -1.0, dr[k]), jnp.where(at_row, 0.0, di[k])
            tr, ti = cr * pr + ci * pi, ci * pr - cr * pi
            factors.append((tr, ti, inverse, tr * inverse, ti * inverse))
        for c in range(k + 1, TILE):
            for (dr, di), (tr, ti, inverse, fr, fi) in zip(columns, factors):
                ar, ai = row_of(dr[c], k), row_of(di[c], k)
                zr, zi = jnp.where(at_row, 0.0, dr[c]), jnp.where(at_row, 0.0, di[c])
                if c == k + 1:
                    dr[c] = zr - (tr * ar - ti * ai) * inverse
                    di[c] = zi - (tr * ai + ti * ar) * inverse
                else:
                    dr[c], di[c] = zr - (fr * ar - fi * ai), zi - (fr * ai + fi * ar)
        for m, ((real, imag), (_, _, _, fr, fi)) in enumerate(zip(pairs, factors)):
            ar = jnp.where(at_lane, 1.0, row_of(real, k))
            ai = jnp.where(at_lane, 0.0, row_of(imag, k))
            pairs[m] = (
                jnp.where(cleared, 0.0, real) - (fr * ar - fi * ai),
                jnp.where(cleared, 0.0, imag) - (fr * ai + fi * ar),
            )
    return pairs


def eliminate_panel(panels, first, row, lane):
    tiles = len(panels[0])
    for s in range(tiles):
        base = first + s * TILE
        others = [(s + 1 + u) % tiles for u in range(tiles - 1)]
        columns = [{t: spread_columns(*panel[t], base) for t in others} for panel in panels]
        done = eliminate_tiles([panel[s] for panel in panels], base, row, lane)
        rows = [[(row_of(real, k), row_of(imag, k)) for k in range(TILE)] for real, imag in done]
        inside = (lane >= base) & (lane < base + TILE)
        for t in others:
            for m, panel in enumerate(panels):
                real, imag = panel[t]
                real, imag = jnp.where(inside, 0.0, real), jnp.where(inside, 0.0, imag)
                for cr, ci, (wr, wi) in zip(*columns[m][t], rows[m]):
                    real, imag = real - (cr * wr - ci * wi), imag - (cr * wi + ci * wr)
                panel[t] = (real, imag)
        for m, panel in enumerate(panels):
            panel[s] = done[m]
    return panels


def invert_in_place(ref, count):
    size = ref.shape[-1]
    width = min(PANEL, size)
    tiles = width // TILE

    def step(j, carry):
        first = j * width
        row = lax.broadcasted_iota(jnp.int32, (TILE, size), 0)
        lane = lax.broadcasted_iota(jnp.int32, (TILE, size), 1)
        panels, lefts, results = [], [], []
        for m in range(count):
            at = [pl.ds(pl.multiple_of(first + t * TILE, TILE), TILE) for t in range(tiles)]
            panels.append([(ref[m, 0, rows, :], ref[m, 1, rows, :]) for rows in at])
            parts = [real for real, _ in panels[m]] + [imag for _, imag in panels[m]]
            lh, lm, ll = three_parts(jnp.concatenate(parts, 0))
            lefts.append(jnp.concatenate([lh, lh, lm, lh, lm, ll], 0))
        panels = eliminate_panel(panels, first, row, lane)
        block = (lane >= first) & (lane < first + width)
        full_lane = lax.broadcasted_iota(jnp.int32, (size, size), 1)
        cleared = (full_lane >= first) & (full_lane < first + width)
        for m in range(count):
            wr = jnp.concatenate([jnp.where(block, -real, real) for real, _ in panels[m]], 0)
            wi = jnp.concatenate([jnp.where(block, -imag, imag) for _, imag in panels[m]], 0)
            rh, rm, rl = three_parts(square(wr, wi))
            change = lax.dot_general(
                lefts[m],
                jnp.concatenate([rh, rm, rh, rl, rm, rh], 0),
                (((0,), (0,)), ((), ())),
                preferred_element_type=f32,
            )
            real = jnp.where(cleared, 0.0, ref[m, 0]) - change[:, :size]
            imag = jnp.where(cleared, 0.0, ref[m, 1]) - change[:, size:]
            results.append((real, imag, wr, wi))
        for m, (real, imag, wr, wi) in enumerate(results):
            rows = pl.ds(pl.multiple_of(first, width), width)
            ref[m, 0] = real
            ref[m, 1] = imag
            ref[m, 0, rows, :] = wr
            ref[m, 1, rows, :] = wi
        return carry

    lax.fori_loop(0, size // width, step, 0)


def wide(real, imag):
    return jnp.concatenate([real, imag], 1)


def square(real, imag):
    return jnp.concatenate([wide(real, imag), wide(-imag, real)], 0)


def packed_half(value):
    size = value.shape[0]
    half = size // 2
    row = lax.broadcasted_iota(jnp.int32, (half, size), 0)
    lane = lax.broadcasted_iota(jnp.int32, (half, size), 1)
    quarters = jnp.where((lane < half) | (lane - half > row), pltpu.roll(value[:half], half, 1), value[half:])
    full_row = lax.broadcasted_iota(jnp.int32, (size, size), 0)
    full_lane = lax.broadcasted_iota(jnp.int32, (size, size), 1)
    diagonal = jnp.sum(jnp.where(full_row == full_lane, value, 0.0), axis=0, keepdims=True)
    return jnp.concatenate([quarters, jnp.broadcast_to(diagonal, (TILE, size))], 0)


def unpacked(packed):
    size = packed.shape[1]
    half = size // 2
    quarters = packed[:half]
    whole = jnp.concatenate([pltpu.roll(quarters, half, 1), quarters], 0)
    row = lax.broadcasted_iota(jnp.int32, (size, size), 0)
    lane = lax.broadcasted_iota(jnp.int32, (size, size), 1)
    as_is = ((row < half) & (lane > row)) | ((row >= half) & (lane >= half) & (lane < row))
    full = jnp.where(as_is, whole, whole.T)
    return jnp.where(row == lane, jnp.broadcast_to(packed[half : half + 1], (size, size)), full)


def exact_dot(left, right, dims):
    (over_left,), (over_right,) = dims
    lh, lm, ll = three_parts(left)
    rh, rm, rl = three_parts(right)
    return lax.dot_general(
        jnp.concatenate([lh, lh, lm, lh, lm, ll], over_left),
        jnp.concatenate([rh, rm, rh, rl, rm, rh], over_right),
        (dims, ((), ())),
        preferred_element_type=f32,
    )


def chain_kernel(count, total_energies, damping_ref, *refs):
    blocks, refs = refs[:count], refs[count:]
    green_ref, packed_ref, slab_ref, diagonal_ref, link_ref, work_ref, arrived = refs
    size = green_ref.shape[-1]
    slab, position = lax.axis_index("slab"), lax.axis_index("energy")
    energy = -4.0 + 8.0 * position.astype(f32) / (total_energies - 1)
    damping = damping_ref[0]
    copies = [
        pltpu.make_async_copy(blocks[d], slab_ref.at[((slab ^ d) - slab) & (count - 1)], arrived.at[d])
        for d in range(count)
    ]
    in_order = list(range(1, count, 2)) + list(range(0, count, 2))
    for d in in_order:
        copies[d].start()
    row = lax.broadcasted_iota(jnp.int32, (size, size), 0)
    lane = lax.broadcasted_iota(jnp.int32, (size, size), 1)
    identity = jnp.where(row == lane, 1.0, 0.0).astype(f32)

    def is_last(step):
        return ((slab + step) & (count - 1)) == count - 1

    def cut_link(step):
        return slab_ref[step, 1] * jnp.where(is_last(step), 0.0, 1.0)

    def place(steps):
        for d in steps:
            copies[d].wait()
        for step in steps:
            diagonal_ref[step, 0] = energy * identity - slab_ref[step, 0]
            diagonal_ref[step, 1] = damping * identity

            @pl.when(is_last(step))
            def _():
                link = slab_ref[step, 1]
                diagonal_ref[step, 1] = diagonal_ref[step, 1] + 0.5 * exact_dot(link, link, ((1,), (1,)))

    def subtract(node, real, imag):
        diagonal_ref[node, 0] = diagonal_ref[node, 0] - real
        diagonal_ref[node, 1] = diagonal_ref[node, 1] - imag

    place(range(1, count, 2))
    for level in range(count.bit_length() - 1):
        stride = 1 << level
        nodes = list(range(0, count, stride))
        odds = nodes[1::2]
        for first in range(0, len(odds), 2):
            group = odds[first : first + 2]
            for m, node in enumerate(group):
                work_ref[m] = diagonal_ref[node]
            invert_in_place(work_ref, len(group))
            if level == 0 and first == 0:
                place(range(0, count, 2))
            for m, node in enumerate(group):
                before, after = node - stride, (node + stride) % count
                middle = (work_ref[m, 0], work_ref[m, 1])
                if level == 0:
                    ends = [(cut_link(before),), (cut_link(node).T,)]
                else:
                    ends = [(link_ref[before, 0], link_ref[before, 1]), (link_ref[node, 0].T, link_ref[node, 1].T)]
                if before == after:
                    ends = [tuple(a + b for a, b in zip(*ends))]
                ends = tuple(jnp.concatenate(parts, 0) for parts in zip(*ends))
                height = ends[0].shape[0]
                if level == 0:
                    both = exact_dot(ends[0], wide(*middle), ((1,), (0,)))
                    both = jnp.concatenate([both[:, :size], both[:, size:]], 0)
                    both = exact_dot(both, ends[0], ((1,), (1,)))
                    real, imag = both[:height], both[height:]
                else:
                    both = exact_dot(wide(*ends), square(*middle), ((1,), (0,)))
                    turned = jnp.concatenate([wide(ends[0], -ends[1]), wide(ends[1], ends[0])], 0)
                    both = exact_dot(both, turned, ((1,), (1,)))
                    real, imag = both[:, :height], both[:, height:]
                subtract(before, -real[:size, :size], -imag[:size, :size])
                if before != after:
                    subtract(after, -real[size:, size:], -imag[size:, size:])
                    link_ref[before, 0] = real[:size, size:]
                    link_ref[before, 1] = imag[:size, size:]
    work_ref[0] = diagonal_ref[0]
    invert_in_place(work_ref, 1)
    for part in range(2):
        value = -work_ref[0, part]
        green_ref[part] = value
        packed_ref[part] = packed_half(value)


def green_of(blocks, damping, total_energies):
    count, size = len(blocks), blocks[0].shape[-1]
    whole = pl.BlockSpec(memory_space=pltpu.VMEM)
    scalar = pl.BlockSpec(memory_space=pltpu.SMEM)
    return pl.pallas_call(
        functools.partial(chain_kernel, count, total_energies),
        out_shape=(
            jax.ShapeDtypeStruct((2, size, size), f32),
            jax.ShapeDtypeStruct((2, size // 2 + TILE, size), f32),
        ),
        in_specs=[scalar] + [pl.BlockSpec(memory_space=pl.ANY)] * count,
        out_specs=(whole, whole),
        scratch_shapes=[
            pltpu.VMEM((count, 2, size, size), f32),
            pltpu.VMEM((count, 2, size, size), f32),
            pltpu.VMEM((count, 2, size, size), f32),
            pltpu.VMEM((2, 2, size, size), f32),
            pltpu.SemaphoreType.DMA((count,)),
        ],
        name="chain",
    )(damping, *blocks)


def polar_kernel(steps, *refs):
    groups = len(steps)
    blocks, (out_ref, held, arrived) = refs[:groups], refs[groups:]
    me = lax.axis_index("energy")
    copies = [
        pltpu.make_async_copy(block, held.at[me ^ step], arrived.at[i])
        for i, (step, block) in enumerate(zip(steps, blocks))
    ]
    for copy in copies:
        copy.start()
    for copy in copies:
        copy.wait()
    real = imag = jnp.zeros(held.shape[2:], f32)
    for first in range(groups):
        inside = first + me < groups
        second = jnp.where(inside, first + me, 0)
        weight = jnp.where(inside, 1.0 / groups, 0.0)
        br, bi = held[first, 0] * weight, held[first, 1] * weight
        ar, ai = held[second, 0], held[second, 1]
        real = real + (ar * br + ai * bi)
        imag = imag + (ai * br - ar * bi)
    out_ref[0] = unpacked(real)
    out_ref[1] = unpacked(imag)


def correlate(packed, groups):
    def swapped(block, step):
        return lax.ppermute(block, "energy", [(s, s ^ step) for s in range(groups)])

    gathered = [(step, swapped(packed, step)) for step in range(groups - 2, 0, -2)]
    gathered.insert(0, (0, packed))
    gathered = gathered + [(step ^ 1, swapped(block, 1)) for step, block in gathered]
    steps, blocks = zip(*gathered)
    size = packed.shape[-1]
    whole = pl.BlockSpec(memory_space=pltpu.VMEM)
    return pl.pallas_call(
        functools.partial(polar_kernel, steps),
        out_shape=jax.ShapeDtypeStruct((2, size, size), f32),
        in_specs=[pl.BlockSpec(memory_space=pl.ANY)] * groups,
        out_specs=whole,
        scratch_shapes=[pltpu.VMEM((groups,) + packed.shape, f32), pltpu.SemaphoreType.DMA((groups,))],
        name="polar",
    )(*blocks)


def correlate_spread(own, groups):
    _, size, _ = own.shape
    spread = own.reshape(2, groups, size * size // groups)
    mixed = lax.all_to_all(spread[None], "energy", split_axis=2, concat_axis=0, tiled=True)[:, :, 0]
    real, imag = mixed[:, 0], mixed[:, 1]
    pieces = []
    for offset in range(groups):
        ar, ai = real[offset:], imag[offset:]
        br, bi = real[: groups - offset], imag[: groups - offset]
        pieces.append(jnp.stack([jnp.sum(ar * br + ai * bi, 0), jnp.sum(ai * br - ar * bi, 0)]))
    result = (jnp.stack(pieces) / groups)[:, :, None, :]
    back = lax.all_to_all(result, "energy", split_axis=0, concat_axis=2, tiled=True)
    return back.reshape(own.shape)


def on_device(h_diag, coupling, broadening):
    slabs = lax.axis_size("slab")
    groups = lax.axis_size("energy")
    size = h_diag.shape[-1]
    own = jnp.concatenate([h_diag, coupling], 0)
    blocks = {0: own}
    for d in list(range(slabs - 1, 0, -2)) + list(range(slabs - 2, 0, -2)):
        blocks[d] = lax.ppermute(own, "slab", [(s, s ^ d) for s in range(slabs)])
    blocks = [blocks[d] for d in range(slabs)]
    green, packed = green_of(blocks, broadening, groups)
    polar = correlate(packed, groups) if groups <= 8 else correlate_spread(green, groups)
    shape = (1, 1, 2, size, size)
    return green.reshape(shape), polar.reshape(shape)


def solution(mesh):
    return jax.shard_map(
        on_device,
        mesh=mesh,
        in_specs=(P("slab", None, None), P("slab", None, None), P("energy")),
        out_specs=(P("energy", "slab", None, None, None), P("energy", "slab", None, None, None)),
        check_vma=False,
    )
```

```python
import functools

import jax
import jax.numpy as jnp
from jax import lax
from jax.experimental import pallas as pl
from jax.experimental.pallas import tpu as pltpu
from jax.sharding import PartitionSpec as P

f32 = jnp.float32
bf16 = jnp.bfloat16
PANEL = 16
TILE = 8


def three_parts(value):
    high = value.astype(bf16)
    rest = value - high.astype(f32)
    middle = rest.astype(bf16)
    low = (rest - middle.astype(f32)).astype(bf16)
    return high, middle, low


def row_of(tile, k):
    return jnp.broadcast_to(tile[k : k + 1, :], tile.shape)


def column_of(tile, k):
    return jnp.broadcast_to(tile[:, k : k + 1], tile.shape)


def lanes_at(tile, index):
    return jnp.take_along_axis(tile, index, axis=1, mode="promise_in_bounds")


def spread_columns(real, imag, base):
    index = [jnp.zeros(real.shape, jnp.int32) + (base + k) for k in range(TILE)]
    return [lanes_at(real, i) for i in index], [lanes_at(imag, i) for i in index]


def eliminate_tiles(pairs, base, row, lane):
    columns = [spread_columns(real, imag, base) for real, imag in pairs]
    pairs = list(pairs)
    for k in range(TILE):
        at_row = row == k
        at_lane = lane == base + k
        cleared = at_row | at_lane
        factors = []
        for dr, di in columns:
            pr, pi = row_of(dr[k], k), row_of(di[k], k)
            inverse = 1.0 / (pr * pr + pi * pi)
            cr, ci = jnp.where(at_row, -1.0, dr[k]), jnp.where(at_row, 0.0, di[k])
            tr, ti = cr * pr + ci * pi, ci * pr - cr * pi
            factors.append((tr, ti, inverse, tr * inverse, ti * inverse))
        for c in range(k + 1, TILE):
            for (dr, di), (tr, ti, inverse, fr, fi) in zip(columns, factors):
                ar, ai = row_of(dr[c], k), row_of(di[c], k)
                zr, zi = jnp.where(at_row, 0.0, dr[c]), jnp.where(at_row, 0.0, di[c])
                if c == k + 1:
                    dr[c] = zr - (tr * ar - ti * ai) * inverse
                    di[c] = zi - (tr * ai + ti * ar) * inverse
                else:
                    dr[c], di[c] = zr - (fr * ar - fi * ai), zi - (fr * ai + fi * ar)
        for m, ((real, imag), (_, _, _, fr, fi)) in enumerate(zip(pairs, factors)):
            ar = jnp.where(at_lane, 1.0, row_of(real, k))
            ai = jnp.where(at_lane, 0.0, row_of(imag, k))
            pairs[m] = (
                jnp.where(cleared, 0.0, real) - (fr * ar - fi * ai),
                jnp.where(cleared, 0.0, imag) - (fr * ai + fi * ar),
            )
    return pairs


def eliminate_panel(panels, first, row, lane):
    tiles = len(panels[0])
    for s in range(tiles):
        base = first + s * TILE
        others = [(s + 1 + u) % tiles for u in range(tiles - 1)]
        columns = [{t: spread_columns(*panel[t], base) for t in others} for panel in panels]
        done = eliminate_tiles([panel[s] for panel in panels], base, row, lane)
        rows = [[(row_of(real, k), row_of(imag, k)) for k in range(TILE)] for real, imag in done]
        inside = (lane >= base) & (lane < base + TILE)
        for t in others:
            for m, panel in enumerate(panels):
                real, imag = panel[t]
                real, imag = jnp.where(inside, 0.0, real), jnp.where(inside, 0.0, imag)
                for cr, ci, (wr, wi) in zip(*columns[m][t], rows[m]):
                    real, imag = real - (cr * wr - ci * wi), imag - (cr * wi + ci * wr)
                panel[t] = (real, imag)
        for m, panel in enumerate(panels):
            panel[s] = done[m]
    return panels


def invert_in_place(ref, count):
    size = ref.shape[-1]
    width = min(PANEL, size)
    tiles = width // TILE

    def step(j, carry):
        first = j * width
        row = lax.broadcasted_iota(jnp.int32, (TILE, size), 0)
        lane = lax.broadcasted_iota(jnp.int32, (TILE, size), 1)
        panels, lefts, results = [], [], []
        for m in range(count):
            at = [pl.ds(pl.multiple_of(first + t * TILE, TILE), TILE) for t in range(tiles)]
            panels.append([(ref[m, 0, rows, :], ref[m, 1, rows, :]) for rows in at])
            parts = [real for real, _ in panels[m]] + [imag for _, imag in panels[m]]
            lh, lm, ll = three_parts(jnp.concatenate(parts, 0))
            lefts.append(jnp.concatenate([lh, lh, lm, lh, lm, ll], 0))
        panels = eliminate_panel(panels, first, row, lane)
        block = (lane >= first) & (lane < first + width)
        full_lane = lax.broadcasted_iota(jnp.int32, (size, size), 1)
        cleared = (full_lane >= first) & (full_lane < first + width)
        for m in range(count):
            wr = jnp.concatenate([jnp.where(block, -real, real) for real, _ in panels[m]], 0)
            wi = jnp.concatenate([jnp.where(block, -imag, imag) for _, imag in panels[m]], 0)
            rh, rm, rl = three_parts(square(wr, wi))
            change = lax.dot_general(
                lefts[m],
                jnp.concatenate([rh, rm, rh, rl, rm, rh], 0),
                (((0,), (0,)), ((), ())),
                preferred_element_type=f32,
            )
            real = jnp.where(cleared, 0.0, ref[m, 0]) - change[:, :size]
            imag = jnp.where(cleared, 0.0, ref[m, 1]) - change[:, size:]
            results.append((real, imag, wr, wi))
        for m, (real, imag, wr, wi) in enumerate(results):
            rows = pl.ds(pl.multiple_of(first, width), width)
            ref[m, 0] = real
            ref[m, 1] = imag
            ref[m, 0, rows, :] = wr
            ref[m, 1, rows, :] = wi
        return carry

    lax.fori_loop(0, size // width, step, 0)


def wide(real, imag):
    return jnp.concatenate([real, imag], 1)


def square(real, imag):
    return jnp.concatenate([wide(real, imag), wide(-imag, real)], 0)


def half_masks(rows, size):
    row = lax.broadcasted_iota(jnp.int32, (rows, size), 0)
    lane = lax.broadcasted_iota(jnp.int32, (rows, size), 1)
    past = lax.rem(lane - row + size, size)
    return past < size // 2, (past == size // 2) & (row < size // 2)


def packed_half(value):
    size = value.shape[0]
    half = size // 2
    kept, middle = half_masks(half, size)
    upper = value[:half]
    extra = jnp.sum(jnp.where(middle, upper, 0.0), axis=0, keepdims=True)
    return jnp.concatenate([jnp.where(kept, upper, value[half:]), jnp.broadcast_to(extra, (TILE, size))], 0)


def unpacked(packed):
    size = packed.shape[1]
    half = size // 2
    kept, middle = half_masks(size, size)
    whole = jnp.concatenate([packed[:half], packed[:half]], 0)
    whole = jnp.where(middle, jnp.broadcast_to(packed[half : half + 1], (size, size)), whole)
    return jnp.where(kept | middle, whole, whole.T)


def exact_dot(left, right, dims):
    (over_left,), (over_right,) = dims
    lh, lm, ll = three_parts(left)
    rh, rm, rl = three_parts(right)
    return lax.dot_general(
        jnp.concatenate([lh, lh, lm, lh, lm, ll], over_left),
        jnp.concatenate([rh, rm, rh, rl, rm, rh], over_right),
        (dims, ((), ())),
        preferred_element_type=f32,
    )


def chain_kernel(count, total_energies, damping_ref, *refs):
    blocks, refs = refs[:count], refs[count:]
    green_ref, packed_ref, slab_ref, diagonal_ref, link_ref, work_ref, arrived = refs
    size = green_ref.shape[-1]
    slab, position = lax.axis_index("slab"), lax.axis_index("energy")
    energy = -4.0 + 8.0 * position.astype(f32) / (total_energies - 1)
    damping = damping_ref[0]
    copies = [
        pltpu.make_async_copy(blocks[d], slab_ref.at[((slab ^ d) - slab) & (count - 1)], arrived.at[d])
        for d in range(count)
    ]
    in_order = list(range(1, count, 2)) + list(range(0, count, 2))
    for d in in_order:
        copies[d].start()
    row = lax.broadcasted_iota(jnp.int32, (size, size), 0)
    lane = lax.broadcasted_iota(jnp.int32, (size, size), 1)
    identity = jnp.where(row == lane, 1.0, 0.0).astype(f32)

    def is_last(step):
        return ((slab + step) & (count - 1)) == count - 1

    def link_of(step):
        return slab_ref[step, size // 2 + TILE :, :]

    def cut_link(step):
        return link_of(step) * jnp.where(is_last(step), 0.0, 1.0)

    def place(steps):
        for d in steps:
            copies[d].wait()
        for step in steps:
            diagonal_ref[step, 0] = energy * identity - unpacked(slab_ref[step, : size // 2 + TILE, :])
            diagonal_ref[step, 1] = damping * identity

            @pl.when(is_last(step))
            def _():
                link = link_of(step)
                diagonal_ref[step, 1] = diagonal_ref[step, 1] + 0.5 * exact_dot(link, link, ((1,), (1,)))

    def subtract(node, real, imag):
        diagonal_ref[node, 0] = diagonal_ref[node, 0] - real
        diagonal_ref[node, 1] = diagonal_ref[node, 1] - imag

    place(range(1, count, 2))
    for level in range(count.bit_length() - 1):
        stride = 1 << level
        nodes = list(range(0, count, stride))
        odds = nodes[1::2]
        for first in range(0, len(odds), 2):
            group = odds[first : first + 2]
            for m, node in enumerate(group):
                work_ref[m] = diagonal_ref[node]
            invert_in_place(work_ref, len(group))
            if level == 0 and first == 0:
                place(range(0, count, 2))
            for m, node in enumerate(group):
                before, after = node - stride, (node + stride) % count
                middle = (work_ref[m, 0], work_ref[m, 1])
                if level == 0:
                    ends = [(cut_link(before),), (cut_link(node).T,)]
                else:
                    ends = [(link_ref[before, 0], link_ref[before, 1]), (link_ref[node, 0].T, link_ref[node, 1].T)]
                if before == after:
                    ends = [tuple(a + b for a, b in zip(*ends))]
                ends = tuple(jnp.concatenate(parts, 0) for parts in zip(*ends))
                height = ends[0].shape[0]
                if level == 0:
                    both = exact_dot(ends[0], wide(*middle), ((1,), (0,)))
                    both = jnp.concatenate([both[:, :size], both[:, size:]], 0)
                    both = exact_dot(both, ends[0], ((1,), (1,)))
                    real, imag = both[:height], both[height:]
                else:
                    both = exact_dot(wide(*ends), square(*middle), ((1,), (0,)))
                    turned = jnp.concatenate([wide(ends[0], -ends[1]), wide(ends[1], ends[0])], 0)
                    both = exact_dot(both, turned, ((1,), (1,)))
                    real, imag = both[:, :height], both[:, height:]
                subtract(before, -real[:size, :size], -imag[:size, :size])
                if before != after:
                    subtract(after, -real[size:, size:], -imag[size:, size:])
                    link_ref[before, 0] = real[:size, size:]
                    link_ref[before, 1] = imag[:size, size:]
    work_ref[0] = diagonal_ref[0]
    invert_in_place(work_ref, 1)
    for part in range(2):
        value = -work_ref[0, part]
        green_ref[part] = value
        packed_ref[part] = packed_half(value)


def green_of(blocks, damping, total_energies):
    count, size = len(blocks), blocks[0].shape[-1]
    whole = pl.BlockSpec(memory_space=pltpu.VMEM)
    scalar = pl.BlockSpec(memory_space=pltpu.SMEM)
    return pl.pallas_call(
        functools.partial(chain_kernel, count, total_energies),
        out_shape=(
            jax.ShapeDtypeStruct((2, size, size), f32),
            jax.ShapeDtypeStruct((2, size // 2 + TILE, size), f32),
        ),
        in_specs=[scalar] + [pl.BlockSpec(memory_space=pltpu.HBM)] * count,
        out_specs=(whole, whole),
        scratch_shapes=[
            pltpu.VMEM((count,) + blocks[0].shape, f32),
            pltpu.VMEM((count, 2, size, size), f32),
            pltpu.VMEM((count, 2, size, size), f32),
            pltpu.VMEM((2, 2, size, size), f32),
            pltpu.SemaphoreType.DMA((count,)),
        ],
        name="chain",
    )(damping, *blocks)


def polar_kernel(steps, *refs):
    groups = len(steps)
    blocks, (out_ref, held, arrived) = refs[:groups], refs[groups:]
    me = lax.axis_index("energy")
    copies = [
        pltpu.make_async_copy(block, held.at[me ^ step], arrived.at[i])
        for i, (step, block) in enumerate(zip(steps, blocks))
    ]
    for copy in copies:
        copy.start()
    for copy in copies:
        copy.wait()
    real = imag = jnp.zeros(held.shape[2:], f32)
    for first in range(groups):
        inside = first + me < groups
        second = jnp.where(inside, first + me, 0)
        weight = jnp.where(inside, 1.0 / groups, 0.0)
        br, bi = held[first, 0] * weight, held[first, 1] * weight
        ar, ai = held[second, 0], held[second, 1]
        real = real + (ar * br + ai * bi)
        imag = imag + (ai * br - ar * bi)
    out_ref[0] = unpacked(real)
    out_ref[1] = unpacked(imag)


def correlate(packed, groups):
    def swapped(block, step):
        return lax.ppermute(block, "energy", [(s, s ^ step) for s in range(groups)])

    gathered = [(step, swapped(packed, step)) for step in range(groups - 2, 0, -2)]
    gathered.insert(0, (0, packed))
    gathered = gathered + [(step ^ 1, swapped(block, 1)) for step, block in gathered]
    steps, blocks = zip(*gathered)
    size = packed.shape[-1]
    whole = pl.BlockSpec(memory_space=pltpu.VMEM)
    return pl.pallas_call(
        functools.partial(polar_kernel, steps),
        out_shape=jax.ShapeDtypeStruct((2, size, size), f32),
        in_specs=[pl.BlockSpec(memory_space=pltpu.HBM)] * groups,
        out_specs=whole,
        scratch_shapes=[pltpu.VMEM((groups,) + packed.shape, f32), pltpu.SemaphoreType.DMA((groups,))],
        name="polar",
    )(*blocks)


def correlate_spread(own, groups):
    _, size, _ = own.shape
    spread = own.reshape(2, groups, size * size // groups)
    mixed = lax.all_to_all(spread[None], "energy", split_axis=2, concat_axis=0, tiled=True)[:, :, 0]
    real, imag = mixed[:, 0], mixed[:, 1]
    pieces = []
    for offset in range(groups):
        ar, ai = real[offset:], imag[offset:]
        br, bi = real[: groups - offset], imag[: groups - offset]
        pieces.append(jnp.stack([jnp.sum(ar * br + ai * bi, 0), jnp.sum(ai * br - ar * bi, 0)]))
    result = (jnp.stack(pieces) / groups)[:, :, None, :]
    back = lax.all_to_all(result, "energy", split_axis=0, concat_axis=2, tiled=True)
    return back.reshape(own.shape)


def on_device(h_diag, coupling, broadening):
    slabs = lax.axis_size("slab")
    groups = lax.axis_size("energy")
    size = h_diag.shape[-1]
    own = jnp.concatenate([packed_half(h_diag[0]), coupling[0]], 0)
    blocks = {0: own}
    for d in list(range(slabs - 1, 0, -2)) + list(range(slabs - 2, 0, -2)):
        blocks[d] = lax.ppermute(own, "slab", [(s, s ^ d) for s in range(slabs)])
    blocks = [blocks[d] for d in range(slabs)]
    green, packed = green_of(blocks, broadening, groups)
    polar = correlate(packed, groups) if groups <= 8 else correlate_spread(green, groups)
    shape = (1, 1, 2, size, size)
    return green.reshape(shape), polar.reshape(shape)


def solution(mesh):
    return jax.shard_map(
        on_device,
        mesh=mesh,
        in_specs=(P("slab", None, None), P("slab", None, None), P("energy")),
        out_specs=(P("energy", "slab", None, None, None), P("energy", "slab", None, None, None)),
        check_vma=False,
    )
```

```python
import functools

import jax
import jax.numpy as jnp
from jax import lax
from jax.experimental import pallas as pl
from jax.experimental.pallas import tpu as pltpu
from jax.sharding import PartitionSpec as P

f32 = jnp.float32
bf16 = jnp.bfloat16
PANEL = 16
TILE = 8
GRANT = 24 << 20


def three_parts(value):
    high = value.astype(bf16)
    rest = value - high.astype(f32)
    middle = rest.astype(bf16)
    low = (rest - middle.astype(f32)).astype(bf16)
    return high, middle, low


def row_of(tile, k):
    return jnp.broadcast_to(tile[k : k + 1, :], tile.shape)


def column_of(tile, k):
    return jnp.broadcast_to(tile[:, k : k + 1], tile.shape)


def lanes_at(tile, index):
    return jnp.take_along_axis(tile, index, axis=1, mode="promise_in_bounds")


def spread_columns(real, imag, base):
    index = [jnp.zeros(real.shape, jnp.int32) + (base + k) for k in range(TILE)]
    return [lanes_at(real, i) for i in index], [lanes_at(imag, i) for i in index]


def eliminate_tiles(pairs, base, row, lane):
    columns = [spread_columns(real, imag, base) for real, imag in pairs]
    pairs = list(pairs)
    for k in range(TILE):
        at_row = row == k
        at_lane = lane == base + k
        cleared = at_row | at_lane
        factors = []
        for dr, di in columns:
            pr, pi = row_of(dr[k], k), row_of(di[k], k)
            inverse = 1.0 / (pr * pr + pi * pi)
            cr, ci = jnp.where(at_row, -1.0, dr[k]), jnp.where(at_row, 0.0, di[k])
            tr, ti = cr * pr + ci * pi, ci * pr - cr * pi
            factors.append((tr, ti, inverse, tr * inverse, ti * inverse))
        for c in range(k + 1, TILE):
            for (dr, di), (tr, ti, inverse, fr, fi) in zip(columns, factors):
                ar, ai = row_of(dr[c], k), row_of(di[c], k)
                zr, zi = jnp.where(at_row, 0.0, dr[c]), jnp.where(at_row, 0.0, di[c])
                if c == k + 1:
                    dr[c] = zr - (tr * ar - ti * ai) * inverse
                    di[c] = zi - (tr * ai + ti * ar) * inverse
                else:
                    dr[c], di[c] = zr - (fr * ar - fi * ai), zi - (fr * ai + fi * ar)
        for m, ((real, imag), (_, _, _, fr, fi)) in enumerate(zip(pairs, factors)):
            ar = jnp.where(at_lane, 1.0, row_of(real, k))
            ai = jnp.where(at_lane, 0.0, row_of(imag, k))
            pairs[m] = (
                jnp.where(cleared, 0.0, real) - (fr * ar - fi * ai),
                jnp.where(cleared, 0.0, imag) - (fr * ai + fi * ar),
            )
    return pairs


def eliminate_panel(panels, first, row, lane):
    tiles = len(panels[0])
    for s in range(tiles):
        base = first + s * TILE
        others = [(s + 1 + u) % tiles for u in range(tiles - 1)]
        columns = [{t: spread_columns(*panel[t], base) for t in others} for panel in panels]
        done = eliminate_tiles([panel[s] for panel in panels], base, row, lane)
        rows = [[(row_of(real, k), row_of(imag, k)) for k in range(TILE)] for real, imag in done]
        inside = (lane >= base) & (lane < base + TILE)
        for t in others:
            for m, panel in enumerate(panels):
                real, imag = panel[t]
                real, imag = jnp.where(inside, 0.0, real), jnp.where(inside, 0.0, imag)
                for cr, ci, (wr, wi) in zip(*columns[m][t], rows[m]):
                    real, imag = real - (cr * wr - ci * wi), imag - (cr * wi + ci * wr)
                panel[t] = (real, imag)
        for m, panel in enumerate(panels):
            panel[s] = done[m]
    return panels


def invert_in_place(ref, count):
    size = ref.shape[-1]
    width = min(PANEL, size)
    tiles = width // TILE

    def step(j, carry):
        first = j * width
        row = lax.broadcasted_iota(jnp.int32, (TILE, size), 0)
        lane = lax.broadcasted_iota(jnp.int32, (TILE, size), 1)
        panels, lefts, results = [], [], []
        for m in range(count):
            at = [pl.ds(pl.multiple_of(first + t * TILE, TILE), TILE) for t in range(tiles)]
            panels.append([(ref[m, 0, rows, :], ref[m, 1, rows, :]) for rows in at])
            parts = [real for real, _ in panels[m]] + [imag for _, imag in panels[m]]
            lh, lm, ll = three_parts(jnp.concatenate(parts, 0))
            lefts.append(jnp.concatenate([lh, lh, lm, lh, lm, ll], 0))
        panels = eliminate_panel(panels, first, row, lane)
        block = (lane >= first) & (lane < first + width)
        full_lane = lax.broadcasted_iota(jnp.int32, (size, size), 1)
        cleared = (full_lane >= first) & (full_lane < first + width)
        for m in range(count):
            wr = jnp.concatenate([jnp.where(block, -real, real) for real, _ in panels[m]], 0)
            wi = jnp.concatenate([jnp.where(block, -imag, imag) for _, imag in panels[m]], 0)
            rh, rm, rl = three_parts(square(wr, wi))
            change = lax.dot_general(
                lefts[m],
                jnp.concatenate([rh, rm, rh, rl, rm, rh], 0),
                (((0,), (0,)), ((), ())),
                preferred_element_type=f32,
            )
            real = jnp.where(cleared, 0.0, ref[m, 0]) - change[:, :size]
            imag = jnp.where(cleared, 0.0, ref[m, 1]) - change[:, size:]
            results.append((real, imag, wr, wi))
        for m, (real, imag, wr, wi) in enumerate(results):
            rows = pl.ds(pl.multiple_of(first, width), width)
            ref[m, 0] = real
            ref[m, 1] = imag
            ref[m, 0, rows, :] = wr
            ref[m, 1, rows, :] = wi
        return carry

    lax.fori_loop(0, size // width, step, 0)


def wide(real, imag):
    return jnp.concatenate([real, imag], 1)


def square(real, imag):
    return jnp.concatenate([wide(real, imag), wide(-imag, real)], 0)


def half_masks(rows, size):
    row = lax.broadcasted_iota(jnp.int32, (rows, size), 0)
    lane = lax.broadcasted_iota(jnp.int32, (rows, size), 1)
    past = lax.rem(lane - row + size, size)
    return past < size // 2, (past == size // 2) & (row < size // 2)


def packed_half(value):
    size = value.shape[0]
    half = size // 2
    kept, middle = half_masks(half, size)
    upper = value[:half]
    extra = jnp.sum(jnp.where(middle, upper, 0.0), axis=0, keepdims=True)
    return jnp.concatenate([jnp.where(kept, upper, value[half:]), jnp.broadcast_to(extra, (TILE, size))], 0)


def unpacked(packed):
    size = packed.shape[1]
    half = size // 2
    kept, middle = half_masks(size, size)
    whole = jnp.concatenate([packed[:half], packed[:half]], 0)
    whole = jnp.where(middle, jnp.broadcast_to(packed[half : half + 1], (size, size)), whole)
    return jnp.where(kept | middle, whole, whole.T)


def exact_dot(left, right, dims):
    (over_left,), (over_right,) = dims
    lh, lm, ll = three_parts(left)
    rh, rm, rl = three_parts(right)
    return lax.dot_general(
        jnp.concatenate([lh, lh, lm, lh, lm, ll], over_left),
        jnp.concatenate([rh, rm, rh, rl, rm, rh], over_right),
        (dims, ((), ())),
        preferred_element_type=f32,
    )


def chain_kernel(count, total_energies, damping_ref, *refs):
    blocks, refs = refs[:count], refs[count:]
    green_ref, packed_ref, slab_ref, diagonal_ref, link_ref, work_ref, arrived = refs
    size = green_ref.shape[-1]
    slab, position = lax.axis_index("slab"), lax.axis_index("energy")
    energy = -4.0 + 8.0 * position.astype(f32) / (total_energies - 1)
    damping = damping_ref[0]
    copies = [
        pltpu.make_async_copy(blocks[d], slab_ref.at[((slab ^ d) - slab) & (count - 1)], arrived.at[d])
        for d in range(count)
    ]
    in_order = list(range(1, count, 2)) + list(range(0, count, 2))
    for d in in_order:
        copies[d].start()
    row = lax.broadcasted_iota(jnp.int32, (size, size), 0)
    lane = lax.broadcasted_iota(jnp.int32, (size, size), 1)
    identity = jnp.where(row == lane, 1.0, 0.0).astype(f32)

    def is_last(step):
        return ((slab + step) & (count - 1)) == count - 1

    def link_of(step):
        return slab_ref[step, size // 2 + TILE :, :]

    def cut_link(step):
        return link_of(step) * jnp.where(is_last(step), 0.0, 1.0)

    def place(steps):
        for d in steps:
            copies[d].wait()
        for step in steps:
            diagonal_ref[step, 0] = energy * identity - unpacked(slab_ref[step, : size // 2 + TILE, :])
            diagonal_ref[step, 1] = damping * identity

            @pl.when(is_last(step))
            def _():
                link = link_of(step)
                diagonal_ref[step, 1] = diagonal_ref[step, 1] + 0.5 * exact_dot(link, link, ((1,), (1,)))

    def subtract(node, real, imag):
        diagonal_ref[node, 0] = diagonal_ref[node, 0] - real
        diagonal_ref[node, 1] = diagonal_ref[node, 1] - imag

    place(range(1, count, 2))
    for level in range(count.bit_length() - 1):
        stride = 1 << level
        nodes = list(range(0, count, stride))
        odds = nodes[1::2]
        for first in range(0, len(odds), 2):
            group = odds[first : first + 2]
            for m, node in enumerate(group):
                work_ref[m] = diagonal_ref[node]
            invert_in_place(work_ref, len(group))
            if level == 0 and first == 0:
                place(range(0, count, 2))
            for m, node in enumerate(group):
                before, after = node - stride, (node + stride) % count
                middle = (work_ref[m, 0], work_ref[m, 1])
                if level == 0:
                    ends = [(cut_link(before),), (cut_link(node).T,)]
                else:
                    ends = [(link_ref[before, 0], link_ref[before, 1]), (link_ref[node, 0].T, link_ref[node, 1].T)]
                if before == after:
                    ends = [tuple(a + b for a, b in zip(*ends))]
                ends = tuple(jnp.concatenate(parts, 0) for parts in zip(*ends))
                height = ends[0].shape[0]
                if level == 0:
                    both = exact_dot(ends[0], wide(*middle), ((1,), (0,)))
                    both = jnp.concatenate([both[:, :size], both[:, size:]], 0)
                    both = exact_dot(both, ends[0], ((1,), (1,)))
                    real, imag = both[:height], both[height:]
                else:
                    both = exact_dot(wide(*ends), square(*middle), ((1,), (0,)))
                    turned = jnp.concatenate([wide(ends[0], -ends[1]), wide(ends[1], ends[0])], 0)
                    both = exact_dot(both, turned, ((1,), (1,)))
                    real, imag = both[:, :height], both[:, height:]
                subtract(before, -real[:size, :size], -imag[:size, :size])
                if before != after:
                    subtract(after, -real[size:, size:], -imag[size:, size:])
                    link_ref[before, 0] = real[:size, size:]
                    link_ref[before, 1] = imag[:size, size:]
    work_ref[0] = diagonal_ref[0]
    invert_in_place(work_ref, 1)
    for part in range(2):
        value = -work_ref[0, part]
        green_ref[part] = value
        packed_ref[part] = packed_half(value)


def green_of(blocks, damping, total_energies):
    count, size = len(blocks), blocks[0].shape[-1]
    whole = pl.BlockSpec(memory_space=pltpu.VMEM)
    scalar = pl.BlockSpec(memory_space=pltpu.SMEM)
    return pl.pallas_call(
        functools.partial(chain_kernel, count, total_energies),
        out_shape=(
            jax.ShapeDtypeStruct((2, size, size), f32),
            jax.ShapeDtypeStruct((2, size // 2 + TILE, size), f32),
        ),
        in_specs=[scalar] + [pl.BlockSpec(memory_space=pl.ANY)] * count,
        out_specs=(whole, whole),
        scratch_shapes=[
            pltpu.VMEM((count,) + blocks[0].shape, f32),
            pltpu.VMEM((count, 2, size, size), f32),
            pltpu.VMEM((count, 2, size, size), f32),
            pltpu.VMEM((2, 2, size, size), f32),
            pltpu.SemaphoreType.DMA((count,)),
        ],
        compiler_params=pltpu.CompilerParams(vmem_limit_bytes=GRANT),
        name="chain",
    )(damping, *blocks)


def polar_kernel(steps, green_ref, *refs):
    groups = len(steps)
    blocks, (green_out_ref, out_ref, held, result, arrived, left) = refs[:groups], refs[groups:]
    me = lax.axis_index("energy")
    copies = [
        pltpu.make_async_copy(block, held.at[me ^ step], arrived.at[i])
        for i, (step, block) in enumerate(zip(steps, blocks))
    ]
    for copy in copies:
        copy.start()
    leaving = [pltpu.make_async_copy(green_ref, green_out_ref, left.at[2])]
    leaving[0].start()
    for copy in copies:
        copy.wait()
    real = imag = jnp.zeros(held.shape[2:], f32)
    for first in range(groups):
        inside = first + me < groups
        second = jnp.where(inside, first + me, 0)
        weight = jnp.where(inside, 1.0 / groups, 0.0)
        br, bi = held[first, 0] * weight, held[first, 1] * weight
        ar, ai = held[second, 0], held[second, 1]
        real = real + (ar * br + ai * bi)
        imag = imag + (ai * br - ar * bi)
    for part, value in enumerate((real, imag)):
        result[part] = unpacked(value)
        leaving.append(pltpu.make_async_copy(result.at[part], out_ref.at[part], left.at[part]))
        leaving[-1].start()
    for copy in leaving:
        copy.wait()


def correlate(green, packed, groups):
    def swapped(block, step):
        return lax.ppermute(block, "energy", [(s, s ^ step) for s in range(groups)])

    gathered = [(step, swapped(packed, step)) for step in range(groups - 2, 0, -2)]
    gathered.insert(0, (0, packed))
    gathered = gathered + [(step ^ 1, swapped(block, 1)) for step, block in gathered]
    steps, blocks = zip(*gathered)
    anywhere = pl.BlockSpec(memory_space=pl.ANY)
    result = jax.ShapeDtypeStruct(green.shape, f32)
    return pl.pallas_call(
        functools.partial(polar_kernel, steps),
        out_shape=(result, result),
        in_specs=[anywhere] * (1 + groups),
        out_specs=(anywhere, anywhere),
        scratch_shapes=[
            pltpu.VMEM((groups,) + packed.shape, f32),
            pltpu.VMEM(green.shape, f32),
            pltpu.SemaphoreType.DMA((groups,)),
            pltpu.SemaphoreType.DMA((3,)),
        ],
        compiler_params=pltpu.CompilerParams(vmem_limit_bytes=GRANT),
        name="polar",
    )(green, *blocks)


def correlate_spread(own, groups):
    _, size, _ = own.shape
    spread = own.reshape(2, groups, size * size // groups)
    mixed = lax.all_to_all(spread[None], "energy", split_axis=2, concat_axis=0, tiled=True)[:, :, 0]
    real, imag = mixed[:, 0], mixed[:, 1]
    pieces = []
    for offset in range(groups):
        ar, ai = real[offset:], imag[offset:]
        br, bi = real[: groups - offset], imag[: groups - offset]
        pieces.append(jnp.stack([jnp.sum(ar * br + ai * bi, 0), jnp.sum(ai * br - ar * bi, 0)]))
    result = (jnp.stack(pieces) / groups)[:, :, None, :]
    back = lax.all_to_all(result, "energy", split_axis=0, concat_axis=2, tiled=True)
    return back.reshape(own.shape)


def on_device(h_diag, coupling, broadening):
    slabs = lax.axis_size("slab")
    groups = lax.axis_size("energy")
    size = h_diag.shape[-1]
    own = jnp.concatenate([packed_half(h_diag[0]), coupling[0]], 0)
    blocks = {0: own}
    for d in list(range(slabs - 1, 0, -2)) + list(range(slabs - 2, 0, -2)):
        blocks[d] = lax.ppermute(own, "slab", [(s, s ^ d) for s in range(slabs)])
    blocks = [blocks[d] for d in range(slabs)]
    green, packed = green_of(blocks, broadening, groups)
    if groups <= 8:
        green, polar = correlate(green, packed, groups)
    else:
        polar = correlate_spread(green, groups)
    shape = (1, 1, 2, size, size)
    return green.reshape(shape), polar.reshape(shape)


def solution(mesh):
    return jax.shard_map(
        on_device,
        mesh=mesh,
        in_specs=(P("slab", None, None), P("slab", None, None), P("energy")),
        out_specs=(P("energy", "slab", None, None, None), P("energy", "slab", None, None, None)),
        check_vma=False,
    )
```

```python
import functools

import jax
import jax.numpy as jnp
from jax import lax
from jax.experimental import pallas as pl
from jax.experimental.pallas import tpu as pltpu
from jax.sharding import PartitionSpec as P

f32 = jnp.float32
bf16 = jnp.bfloat16
PANEL = 32
TILE = 8
GRANT = 24 << 20


def three_parts(value):
    high = value.astype(bf16)
    rest = value - high.astype(f32)
    middle = rest.astype(bf16)
    low = (rest - middle.astype(f32)).astype(bf16)
    return high, middle, low


def row_of(tile, k):
    return jnp.broadcast_to(tile[k : k + 1, :], tile.shape)


def column_of(tile, k):
    return jnp.broadcast_to(tile[:, k : k + 1], tile.shape)


def lanes_at(tile, index):
    return jnp.take_along_axis(tile, index, axis=1, mode="promise_in_bounds")


def spread_columns(real, imag, base):
    index = [jnp.zeros(real.shape, jnp.int32) + (base + k) for k in range(TILE)]
    return [lanes_at(real, i) for i in index], [lanes_at(imag, i) for i in index]


def eliminate_tiles(pairs, base, row, lane):
    columns = [spread_columns(real, imag, base) for real, imag in pairs]
    pairs = list(pairs)
    for k in range(TILE):
        at_row = row == k
        at_lane = lane == base + k
        cleared = at_row | at_lane
        factors = []
        for dr, di in columns:
            pr, pi = row_of(dr[k], k), row_of(di[k], k)
            inverse = 1.0 / (pr * pr + pi * pi)
            cr, ci = jnp.where(at_row, -1.0, dr[k]), jnp.where(at_row, 0.0, di[k])
            tr, ti = cr * pr + ci * pi, ci * pr - cr * pi
            factors.append((tr, ti, inverse, tr * inverse, ti * inverse))
        for c in range(k + 1, TILE):
            for (dr, di), (tr, ti, inverse, fr, fi) in zip(columns, factors):
                ar, ai = row_of(dr[c], k), row_of(di[c], k)
                zr, zi = jnp.where(at_row, 0.0, dr[c]), jnp.where(at_row, 0.0, di[c])
                if c == k + 1:
                    dr[c] = zr - (tr * ar - ti * ai) * inverse
                    di[c] = zi - (tr * ai + ti * ar) * inverse
                else:
                    dr[c], di[c] = zr - (fr * ar - fi * ai), zi - (fr * ai + fi * ar)
        for m, ((real, imag), (_, _, _, fr, fi)) in enumerate(zip(pairs, factors)):
            ar = jnp.where(at_lane, 1.0, row_of(real, k))
            ai = jnp.where(at_lane, 0.0, row_of(imag, k))
            pairs[m] = (
                jnp.where(cleared, 0.0, real) - (fr * ar - fi * ai),
                jnp.where(cleared, 0.0, imag) - (fr * ai + fi * ar),
            )
    return pairs


def times(left, right):
    return left[0] * right[0] - left[1] * right[1], left[0] * right[1] + left[1] * right[0]


def minus(left, right):
    return left[0] - right[0], left[1] - right[1]


def eliminate_tiles_by_pairs(pairs, base, row, lane):
    columns = [spread_columns(real, imag, base) for real, imag in pairs]
    pairs = list(pairs)
    for k in range(0, TILE, 2):
        first, second = row == k, row == k + 1
        both_rows = first | second
        first_lane, second_lane = lane == base + k, lane == base + k + 1
        both_lanes = first_lane | second_lane
        cleared = both_rows | both_lanes
        ones = (jnp.where(first_lane, 1.0, 0.0), jnp.where(second_lane, 1.0, 0.0))
        factors = []
        for dr, di in columns:
            p00, p10 = [(row_of(dr[k], r), row_of(di[k], r)) for r in (k, k + 1)]
            p01, p11 = [(row_of(dr[k + 1], r), row_of(di[k + 1], r)) for r in (k, k + 1)]
            det = minus(times(p00, p11), times(p01, p10))
            inverse = 1.0 / (det[0] * det[0] + det[1] * det[1])
            conjugate = (det[0], -det[1])
            c0, c1 = [
                (
                    jnp.where(both_rows, jnp.where(own, -1.0, 0.0), dr[k + i]),
                    jnp.where(both_rows, 0.0, di[k + i]),
                )
                for i, own in enumerate((first, second))
            ]
            t0 = times(minus(times(c0, p11), times(c1, p10)), conjugate)
            t1 = times(minus(times(c1, p00), times(c0, p01)), conjugate)
            scaled = [(t[0] * inverse, t[1] * inverse) for t in (t0, t1)]
            factors.append((t0, t1, inverse, *scaled))

        def change(f0, f1, a0, a1):
            w0, w1 = times(f0, a0), times(f1, a1)
            return w0[0] + w1[0], w0[1] + w1[1]

        for c in range(k + 2, TILE):
            for (dr, di), (t0, t1, inverse, f0, f1) in zip(columns, factors):
                a0, a1 = [(row_of(dr[c], r), row_of(di[c], r)) for r in (k, k + 1)]
                zr, zi = jnp.where(both_rows, 0.0, dr[c]), jnp.where(both_rows, 0.0, di[c])
                if c < k + 4:
                    w = change(t0, t1, a0, a1)
                    dr[c], di[c] = zr - w[0] * inverse, zi - w[1] * inverse
                else:
                    w = change(f0, f1, a0, a1)
                    dr[c], di[c] = zr - w[0], zi - w[1]
        for m, ((real, imag), (_, _, _, f0, f1)) in enumerate(zip(pairs, factors)):
            a0, a1 = [
                (jnp.where(both_lanes, one, row_of(real, r)), jnp.where(both_lanes, 0.0, row_of(imag, r)))
                for one, r in zip(ones, (k, k + 1))
            ]
            w = change(f0, f1, a0, a1)
            pairs[m] = (jnp.where(cleared, 0.0, real) - w[0], jnp.where(cleared, 0.0, imag) - w[1])
    return pairs


def eliminate_panel(panels, first, row, lane):
    tiles = len(panels[0])
    for s in range(tiles):
        base = first + s * TILE
        others = [(s + 1 + u) % tiles for u in range(tiles - 1)]
        columns = [{t: spread_columns(*panel[t], base) for t in others} for panel in panels]
        eliminate = eliminate_tiles_by_pairs if len(panels) == 1 else eliminate_tiles
        done = eliminate([panel[s] for panel in panels], base, row, lane)
        rows = [[(row_of(real, k), row_of(imag, k)) for k in range(TILE)] for real, imag in done]
        inside = (lane >= base) & (lane < base + TILE)
        for t in others:
            for m, panel in enumerate(panels):
                real, imag = panel[t]
                real, imag = jnp.where(inside, 0.0, real), jnp.where(inside, 0.0, imag)
                for cr, ci, (wr, wi) in zip(*columns[m][t], rows[m]):
                    real, imag = real - (cr * wr - ci * wi), imag - (cr * wi + ci * wr)
                panel[t] = (real, imag)
        for m, panel in enumerate(panels):
            panel[s] = done[m]
    return panels


def invert_in_place(ref, count, unrolled):
    size = ref.shape[-1]
    width = min(PANEL // count, size)
    tiles = width // TILE

    def step(j, carry):
        first = j * width
        row = lax.broadcasted_iota(jnp.int32, (TILE, size), 0)
        lane = lax.broadcasted_iota(jnp.int32, (TILE, size), 1)
        panels, lefts, results = [], [], []
        for m in range(count):
            at = [pl.ds(pl.multiple_of(first + t * TILE, TILE), TILE) for t in range(tiles)]
            panels.append([(ref[m, 0, rows, :], ref[m, 1, rows, :]) for rows in at])
            parts = [real for real, _ in panels[m]] + [imag for _, imag in panels[m]]
            lh, lm, ll = three_parts(jnp.concatenate(parts, 0))
            lefts.append(jnp.concatenate([lh, lh, lm, lh, lm, ll], 0))
        panels = eliminate_panel(panels, first, row, lane)
        block = (lane >= first) & (lane < first + width)
        full_lane = lax.broadcasted_iota(jnp.int32, (size, size), 1)
        cleared = (full_lane >= first) & (full_lane < first + width)
        for m in range(count):
            wr = jnp.concatenate([jnp.where(block, -real, real) for real, _ in panels[m]], 0)
            wi = jnp.concatenate([jnp.where(block, -imag, imag) for _, imag in panels[m]], 0)
            rh, rm, rl = three_parts(square(wr, wi))
            change = lax.dot_general(
                lefts[m],
                jnp.concatenate([rh, rm, rh, rl, rm, rh], 0),
                (((0,), (0,)), ((), ())),
                preferred_element_type=f32,
            )
            real = jnp.where(cleared, 0.0, ref[m, 0]) - change[:, :size]
            imag = jnp.where(cleared, 0.0, ref[m, 1]) - change[:, size:]
            results.append((real, imag, wr, wi))
        for m, (real, imag, wr, wi) in enumerate(results):
            rows = pl.ds(pl.multiple_of(first, width), width)
            ref[m, 0] = real
            ref[m, 1] = imag
            ref[m, 0, rows, :] = wr
            ref[m, 1, rows, :] = wi
        return carry

    lax.fori_loop(0, size // width, step, 0, unroll=size // width if unrolled else 1)


def wide(real, imag):
    return jnp.concatenate([real, imag], 1)


def square(real, imag):
    return jnp.concatenate([wide(real, imag), wide(-imag, real)], 0)


def half_masks(rows, size):
    row = lax.broadcasted_iota(jnp.int32, (rows, size), 0)
    lane = lax.broadcasted_iota(jnp.int32, (rows, size), 1)
    past = lax.rem(lane - row + size, size)
    return past < size // 2, (past == size // 2) & (row < size // 2)


def packed_half(value):
    size = value.shape[0]
    half = size // 2
    kept, middle = half_masks(half, size)
    upper = value[:half]
    extra = jnp.sum(jnp.where(middle, upper, 0.0), axis=0, keepdims=True)
    return jnp.where(kept, upper, value[half:]), jnp.broadcast_to(extra, (TILE, size))


def unpacked(packed, extra):
    size = packed.shape[1]
    kept, middle = half_masks(size, size)
    whole = jnp.concatenate([packed, packed], 0)
    whole = jnp.where(middle, jnp.broadcast_to(extra, (size, size)), whole)
    return jnp.where(kept | middle, whole, whole.T)


def exact_dot(left, right, dims):
    (over_left,), (over_right,) = dims
    lh, lm, ll = three_parts(left)
    rh, rm, rl = three_parts(right)
    return lax.dot_general(
        jnp.concatenate([lh, lh, lm, lh, lm, ll], over_left),
        jnp.concatenate([rh, rm, rh, rl, rm, rh], over_right),
        (dims, ((), ())),
        preferred_element_type=f32,
    )


def chain_kernel(count, total_energies, damping_ref, *refs):
    blocks, refs = refs[:count], refs[count:]
    green_ref, packed_ref, slab_ref, diagonal_ref, link_ref, work_ref, arrived = refs
    size = green_ref.shape[-1]
    slab, position = lax.axis_index("slab"), lax.axis_index("energy")
    energy = -4.0 + 8.0 * position.astype(f32) / (total_energies - 1)
    damping = damping_ref[0]
    copies = [
        pltpu.make_async_copy(blocks[d], slab_ref.at[((slab ^ d) - slab) & (count - 1)], arrived.at[d])
        for d in range(count)
    ]
    in_order = list(range(1, count, 2)) + list(range(0, count, 2))
    for d in in_order:
        copies[d].start()
    row = lax.broadcasted_iota(jnp.int32, (size, size), 0)
    lane = lax.broadcasted_iota(jnp.int32, (size, size), 1)
    identity = jnp.where(row == lane, 1.0, 0.0).astype(f32)

    def is_last(step):
        return ((slab + step) & (count - 1)) == count - 1

    def link_of(step):
        return slab_ref[step, size // 2 + TILE :, :]

    def cut_link(step):
        return link_of(step) * jnp.where(is_last(step), 0.0, 1.0)

    def place(steps):
        for d in steps:
            copies[d].wait()
        for step in steps:
            diagonal_ref[step, 0] = energy * identity - unpacked(
                slab_ref[step, : size // 2, :], slab_ref[step, size // 2 : size // 2 + 1, :]
            )
            diagonal_ref[step, 1] = damping * identity

            @pl.when(is_last(step))
            def _():
                link = link_of(step)
                diagonal_ref[step, 1] = diagonal_ref[step, 1] + 0.5 * exact_dot(link, link, ((1,), (1,)))

    def subtract(node, real, imag):
        diagonal_ref[node, 0] = diagonal_ref[node, 0] - real
        diagonal_ref[node, 1] = diagonal_ref[node, 1] - imag

    place(range(1, count, 2))
    for level in range(count.bit_length() - 1):
        stride = 1 << level
        nodes = list(range(0, count, stride))
        odds = nodes[1::2]
        for first in range(0, len(odds), 2):
            group = odds[first : first + 2]
            for m, node in enumerate(group):
                work_ref[m] = diagonal_ref[node]
            invert_in_place(work_ref, len(group), count <= 4)
            if level == 0 and first == 0:
                place(range(0, count, 2))
            for m, node in enumerate(group):
                before, after = node - stride, (node + stride) % count
                middle = (work_ref[m, 0], work_ref[m, 1])
                if level == 0:
                    ends = [(cut_link(before),), (cut_link(node).T,)]
                else:
                    ends = [(link_ref[before, 0], link_ref[before, 1]), (link_ref[node, 0].T, link_ref[node, 1].T)]
                if before == after:
                    ends = [tuple(a + b for a, b in zip(*ends))]
                ends = tuple(jnp.concatenate(parts, 0) for parts in zip(*ends))
                height = ends[0].shape[0]
                if level == 0:
                    both = exact_dot(ends[0], wide(*middle), ((1,), (0,)))
                    both = jnp.concatenate([both[:, :size], both[:, size:]], 0)
                    both = exact_dot(both, ends[0], ((1,), (1,)))
                    real, imag = both[:height], both[height:]
                else:
                    both = exact_dot(wide(*ends), square(*middle), ((1,), (0,)))
                    turned = jnp.concatenate([wide(ends[0], -ends[1]), wide(ends[1], ends[0])], 0)
                    both = exact_dot(both, turned, ((1,), (1,)))
                    real, imag = both[:, :height], both[:, height:]
                subtract(before, -real[:size, :size], -imag[:size, :size])
                if before != after:
                    subtract(after, -real[size:, size:], -imag[size:, size:])
                    link_ref[before, 0] = real[:size, size:]
                    link_ref[before, 1] = imag[:size, size:]
    work_ref[0] = diagonal_ref[0]
    invert_in_place(work_ref, 1, count <= 4)
    extras = []
    for part in range(2):
        value = -work_ref[0, part]
        green_ref[part] = value
        packed_ref[part * size // 2 : (part + 1) * size // 2, :], extra = packed_half(value)
        extras.append(extra)
    which = lax.broadcasted_iota(jnp.int32, (TILE, size), 0)
    packed_ref[size:, :] = jnp.where(which == 0, extras[0], extras[1])


def green_of(blocks, damping, total_energies):
    count, size = len(blocks), blocks[0].shape[-1]
    whole = pl.BlockSpec(memory_space=pltpu.VMEM)
    scalar = pl.BlockSpec(memory_space=pltpu.SMEM)
    return pl.pallas_call(
        functools.partial(chain_kernel, count, total_energies),
        out_shape=(
            jax.ShapeDtypeStruct((2, size, size), f32),
            jax.ShapeDtypeStruct((size + TILE, size), f32),
        ),
        in_specs=[scalar] + [pl.BlockSpec(memory_space=pl.ANY)] * count,
        out_specs=(whole, whole),
        scratch_shapes=[
            pltpu.VMEM((count,) + blocks[0].shape, f32),
            pltpu.VMEM((count, 2, size, size), f32),
            pltpu.VMEM((count, 2, size, size), f32),
            pltpu.VMEM((2, 2, size, size), f32),
            pltpu.SemaphoreType.DMA((count,)),
        ],
        compiler_params=pltpu.CompilerParams(vmem_limit_bytes=GRANT),
        name="chain",
    )(damping, *blocks)


def polar_kernel(steps, green_ref, *refs):
    groups = len(steps)
    blocks, (green_out_ref, out_ref, held, result, arrived, left) = refs[:groups], refs[groups:]
    me = lax.axis_index("energy")
    copies = [
        pltpu.make_async_copy(block, held.at[me ^ step], arrived.at[i])
        for i, (step, block) in enumerate(zip(steps, blocks))
    ]
    for copy in copies:
        copy.start()
    leaving = [pltpu.make_async_copy(green_ref, green_out_ref, left.at[2])]
    leaving[0].start()
    for copy in copies:
        copy.wait()
    size = held.shape[-1]
    half = size // 2
    real = imag = jnp.zeros((half, size), f32)
    extra_real = extra_imag = jnp.zeros((TILE, size), f32)
    for first in range(groups):
        inside = first + me < groups
        second = jnp.where(inside, first + me, 0)
        weight = jnp.where(inside, 1.0 / groups, 0.0)
        br, bi = held[first, :half, :] * weight, held[first, half:size, :] * weight
        ar, ai = held[second, :half, :], held[second, half:size, :]
        real = real + (ar * br + ai * bi)
        imag = imag + (ai * br - ar * bi)
        b, a = held[first, size:, :] * weight, held[second, size:, :]
        br, bi, ar, ai = row_of(b, 0), row_of(b, 1), row_of(a, 0), row_of(a, 1)
        extra_real = extra_real + (ar * br + ai * bi)
        extra_imag = extra_imag + (ai * br - ar * bi)
    for part, (value, extra) in enumerate(((real, extra_real), (imag, extra_imag))):
        result[part] = unpacked(value, extra[:1])
        leaving.append(pltpu.make_async_copy(result.at[part], out_ref.at[part], left.at[part]))
        leaving[-1].start()
    for copy in leaving:
        copy.wait()


def correlate(green, packed, groups):
    def swapped(block, step):
        return lax.ppermute(block, "energy", [(s, s ^ step) for s in range(groups)])

    gathered = [(step, swapped(packed, step)) for step in range(groups - 2, 0, -2)]
    gathered.insert(0, (0, packed))
    gathered = gathered + [(step ^ 1, swapped(block, 1)) for step, block in gathered]
    steps, blocks = zip(*gathered)
    anywhere = pl.BlockSpec(memory_space=pl.ANY)
    result = jax.ShapeDtypeStruct(green.shape, f32)
    return pl.pallas_call(
        functools.partial(polar_kernel, steps),
        out_shape=(result, result),
        in_specs=[anywhere] * (1 + groups),
        out_specs=(anywhere, anywhere),
        scratch_shapes=[
            pltpu.VMEM((groups,) + packed.shape, f32),
            pltpu.VMEM(green.shape, f32),
            pltpu.SemaphoreType.DMA((groups,)),
            pltpu.SemaphoreType.DMA((3,)),
        ],
        compiler_params=pltpu.CompilerParams(vmem_limit_bytes=GRANT),
        name="polar",
    )(green, *blocks)


def correlate_spread(own, groups):
    _, size, _ = own.shape
    spread = own.reshape(2, groups, size * size // groups)
    mixed = lax.all_to_all(spread[None], "energy", split_axis=2, concat_axis=0, tiled=True)[:, :, 0]
    real, imag = mixed[:, 0], mixed[:, 1]
    pieces = []
    for offset in range(groups):
        ar, ai = real[offset:], imag[offset:]
        br, bi = real[: groups - offset], imag[: groups - offset]
        pieces.append(jnp.stack([jnp.sum(ar * br + ai * bi, 0), jnp.sum(ai * br - ar * bi, 0)]))
    result = (jnp.stack(pieces) / groups)[:, :, None, :]
    back = lax.all_to_all(result, "energy", split_axis=0, concat_axis=2, tiled=True)
    return back.reshape(own.shape)


def on_device(h_diag, coupling, broadening):
    slabs = lax.axis_size("slab")
    groups = lax.axis_size("energy")
    size = h_diag.shape[-1]
    own = jnp.concatenate([*packed_half(h_diag[0]), coupling[0]], 0)
    blocks = {0: own}
    for d in list(range(slabs - 1, 0, -2)) + list(range(slabs - 2, 0, -2)):
        blocks[d] = lax.ppermute(own, "slab", [(s, s ^ d) for s in range(slabs)])
    blocks = [blocks[d] for d in range(slabs)]
    green, packed = green_of(blocks, broadening, groups)
    if groups <= 8:
        green, polar = correlate(green, packed, groups)
    else:
        polar = correlate_spread(green, groups)
    shape = (1, 1, 2, size, size)
    return green.reshape(shape), polar.reshape(shape)


def solution(mesh):
    return jax.shard_map(
        on_device,
        mesh=mesh,
        in_specs=(P("slab", None, None), P("slab", None, None), P("energy")),
        out_specs=(P("energy", "slab", None, None, None), P("energy", "slab", None, None, None)),
        check_vma=False,
    )
```

```python
import functools

import jax
import jax.numpy as jnp
from jax import lax
from jax.experimental import pallas as pl
from jax.experimental.pallas import tpu as pltpu
from jax.sharding import PartitionSpec as P

f32 = jnp.float32
bf16 = jnp.bfloat16
PANEL = 32
TILE = 8
GRANT = 24 << 20


def three_parts(value):
    high = value.astype(bf16)
    rest = value - high.astype(f32)
    middle = rest.astype(bf16)
    low = (rest - middle.astype(f32)).astype(bf16)
    return high, middle, low


def row_of(tile, k):
    return jnp.broadcast_to(tile[k : k + 1, :], tile.shape)


def column_of(tile, k):
    return jnp.broadcast_to(tile[:, k : k + 1], tile.shape)


def lanes_at(tile, index):
    return jnp.take_along_axis(tile, index, axis=1, mode="promise_in_bounds")


def spread_columns(real, imag, base):
    index = [jnp.zeros(real.shape, jnp.int32) + (base + k) for k in range(TILE)]
    return [lanes_at(real, i) for i in index], [lanes_at(imag, i) for i in index]


def eliminate_tiles(pairs, base, row, lane):
    columns = [spread_columns(real, imag, base) for real, imag in pairs]
    pairs = list(pairs)
    for k in range(TILE):
        at_row = row == k
        at_lane = lane == base + k
        cleared = at_row | at_lane
        factors = []
        for dr, di in columns:
            pr, pi = row_of(dr[k], k), row_of(di[k], k)
            inverse = 1.0 / (pr * pr + pi * pi)
            cr, ci = jnp.where(at_row, -1.0, dr[k]), jnp.where(at_row, 0.0, di[k])
            tr, ti = cr * pr + ci * pi, ci * pr - cr * pi
            factors.append((tr, ti, inverse, tr * inverse, ti * inverse))
        for c in range(k + 1, TILE):
            for (dr, di), (tr, ti, inverse, fr, fi) in zip(columns, factors):
                ar, ai = row_of(dr[c], k), row_of(di[c], k)
                zr, zi = jnp.where(at_row, 0.0, dr[c]), jnp.where(at_row, 0.0, di[c])
                if c == k + 1:
                    dr[c] = zr - (tr * ar - ti * ai) * inverse
                    di[c] = zi - (tr * ai + ti * ar) * inverse
                else:
                    dr[c], di[c] = zr - (fr * ar - fi * ai), zi - (fr * ai + fi * ar)
        for m, ((real, imag), (_, _, _, fr, fi)) in enumerate(zip(pairs, factors)):
            ar = jnp.where(at_lane, 1.0, row_of(real, k))
            ai = jnp.where(at_lane, 0.0, row_of(imag, k))
            pairs[m] = (
                jnp.where(cleared, 0.0, real) - (fr * ar - fi * ai),
                jnp.where(cleared, 0.0, imag) - (fr * ai + fi * ar),
            )
    return pairs


def times(left, right):
    return left[0] * right[0] - left[1] * right[1], left[0] * right[1] + left[1] * right[0]


def minus(left, right):
    return left[0] - right[0], left[1] - right[1]


def eliminate_tiles_by_pairs(pairs, base, row, lane):
    columns = [spread_columns(real, imag, base) for real, imag in pairs]
    pairs = list(pairs)
    for k in range(0, TILE, 2):
        first, second = row == k, row == k + 1
        both_rows = first | second
        first_lane, second_lane = lane == base + k, lane == base + k + 1
        both_lanes = first_lane | second_lane
        cleared = both_rows | both_lanes
        ones = (jnp.where(first_lane, 1.0, 0.0), jnp.where(second_lane, 1.0, 0.0))
        factors = []
        for dr, di in columns:
            p00, p10 = [(row_of(dr[k], r), row_of(di[k], r)) for r in (k, k + 1)]
            p01, p11 = [(row_of(dr[k + 1], r), row_of(di[k + 1], r)) for r in (k, k + 1)]
            det = minus(times(p00, p11), times(p01, p10))
            inverse = 1.0 / (det[0] * det[0] + det[1] * det[1])
            conjugate = (det[0], -det[1])
            c0, c1 = [
                (
                    jnp.where(both_rows, jnp.where(own, -1.0, 0.0), dr[k + i]),
                    jnp.where(both_rows, 0.0, di[k + i]),
                )
                for i, own in enumerate((first, second))
            ]
            t0 = times(minus(times(c0, p11), times(c1, p10)), conjugate)
            t1 = times(minus(times(c1, p00), times(c0, p01)), conjugate)
            scaled = [(t[0] * inverse, t[1] * inverse) for t in (t0, t1)]
            factors.append((t0, t1, inverse, *scaled))

        def change(f0, f1, a0, a1):
            w0, w1 = times(f0, a0), times(f1, a1)
            return w0[0] + w1[0], w0[1] + w1[1]

        for c in range(k + 2, TILE):
            for (dr, di), (t0, t1, inverse, f0, f1) in zip(columns, factors):
                a0, a1 = [(row_of(dr[c], r), row_of(di[c], r)) for r in (k, k + 1)]
                zr, zi = jnp.where(both_rows, 0.0, dr[c]), jnp.where(both_rows, 0.0, di[c])
                if c < k + 4:
                    w = change(t0, t1, a0, a1)
                    dr[c], di[c] = zr - w[0] * inverse, zi - w[1] * inverse
                else:
                    w = change(f0, f1, a0, a1)
                    dr[c], di[c] = zr - w[0], zi - w[1]
        for m, ((real, imag), (_, _, _, f0, f1)) in enumerate(zip(pairs, factors)):
            a0, a1 = [
                (jnp.where(both_lanes, one, row_of(real, r)), jnp.where(both_lanes, 0.0, row_of(imag, r)))
                for one, r in zip(ones, (k, k + 1))
            ]
            w = change(f0, f1, a0, a1)
            pairs[m] = (jnp.where(cleared, 0.0, real) - w[0], jnp.where(cleared, 0.0, imag) - w[1])
    return pairs


def eliminate_panel(panels, first, row, lane):
    tiles = len(panels[0])
    for s in range(tiles):
        base = first + s * TILE
        others = [(s + 1 + u) % tiles for u in range(tiles - 1)]
        columns = [{t: spread_columns(*panel[t], base) for t in others} for panel in panels]
        eliminate = eliminate_tiles_by_pairs if len(panels) == 1 else eliminate_tiles
        done = eliminate([panel[s] for panel in panels], base, row, lane)
        rows = [[(row_of(real, k), row_of(imag, k)) for k in range(TILE)] for real, imag in done]
        inside = (lane >= base) & (lane < base + TILE)
        for t in others:
            for m, panel in enumerate(panels):
                real, imag = panel[t]
                real, imag = jnp.where(inside, 0.0, real), jnp.where(inside, 0.0, imag)
                for cr, ci, (wr, wi) in zip(*columns[m][t], rows[m]):
                    real, imag = real - (cr * wr - ci * wi), imag - (cr * wi + ci * wr)
                panel[t] = (real, imag)
        for m, panel in enumerate(panels):
            panel[s] = done[m]
    return panels


def invert_in_place(ref, count, unrolled):
    size = ref.shape[-1]
    width = min(PANEL // count, size)
    tiles = width // TILE

    def step(j, carry):
        first = j * width
        row = lax.broadcasted_iota(jnp.int32, (TILE, size), 0)
        lane = lax.broadcasted_iota(jnp.int32, (TILE, size), 1)
        panels, lefts, results = [], [], []
        for m in range(count):
            at = [pl.ds(pl.multiple_of(first + t * TILE, TILE), TILE) for t in range(tiles)]
            panels.append([(ref[m, 0, rows, :], ref[m, 1, rows, :]) for rows in at])
            parts = [real for real, _ in panels[m]] + [imag for _, imag in panels[m]]
            lh, lm, ll = three_parts(jnp.concatenate(parts, 0))
            lefts.append(jnp.concatenate([lh, lh, lm, lh, lm, ll], 0))
        panels = eliminate_panel(panels, first, row, lane)
        block = (lane >= first) & (lane < first + width)
        full_lane = lax.broadcasted_iota(jnp.int32, (size, size), 1)
        cleared = (full_lane >= first) & (full_lane < first + width)
        for m in range(count):
            wr = jnp.concatenate([jnp.where(block, -real, real) for real, _ in panels[m]], 0)
            wi = jnp.concatenate([jnp.where(block, -imag, imag) for _, imag in panels[m]], 0)
            rh, rm, rl = three_parts(square(wr, wi))
            change = lax.dot_general(
                lefts[m],
                jnp.concatenate([rh, rm, rh, rl, rm, rh], 0),
                (((0,), (0,)), ((), ())),
                preferred_element_type=f32,
            )
            real = jnp.where(cleared, 0.0, ref[m, 0]) - change[:, :size]
            imag = jnp.where(cleared, 0.0, ref[m, 1]) - change[:, size:]
            results.append((real, imag, wr, wi))
        for m, (real, imag, wr, wi) in enumerate(results):
            rows = pl.ds(pl.multiple_of(first, width), width)
            ref[m, 0] = real
            ref[m, 1] = imag
            ref[m, 0, rows, :] = wr
            ref[m, 1, rows, :] = wi
        return carry

    lax.fori_loop(0, size // width, step, 0, unroll=size // width if unrolled else 1)


def wide(real, imag):
    return jnp.concatenate([real, imag], 1)


def square(real, imag):
    return jnp.concatenate([wide(real, imag), wide(-imag, real)], 0)


def half_masks(rows, size):
    row = lax.broadcasted_iota(jnp.int32, (rows, size), 0)
    lane = lax.broadcasted_iota(jnp.int32, (rows, size), 1)
    past = lax.rem(lane - row + size, size)
    return past < size // 2, (past == size // 2) & (row < size // 2)


def packed_half(value):
    size = value.shape[0]
    half = size // 2
    kept, middle = half_masks(half, size)
    upper = value[:half]
    extra = jnp.sum(jnp.where(middle, upper, 0.0), axis=0, keepdims=True)
    return jnp.where(kept, upper, value[half:]), jnp.broadcast_to(extra, (TILE, size))


def unpacked(packed, extra):
    size = packed.shape[1]
    kept, middle = half_masks(size, size)
    whole = jnp.concatenate([packed, packed], 0)
    whole = jnp.where(middle, jnp.broadcast_to(extra, (size, size)), whole)
    return jnp.where(kept | middle, whole, whole.T)


def exact_dot(left, right, dims):
    (over_left,), (over_right,) = dims
    lh, lm, ll = three_parts(left)
    rh, rm, rl = three_parts(right)
    return lax.dot_general(
        jnp.concatenate([lh, lh, lm, lh, lm, ll], over_left),
        jnp.concatenate([rh, rm, rh, rl, rm, rh], over_right),
        (dims, ((), ())),
        preferred_element_type=f32,
    )


def chain_kernel(count, total_energies, damping_ref, *refs):
    blocks, refs = refs[:count], refs[count:]
    green_ref, packed_ref, slab_ref, diagonal_ref, link_ref, work_ref = refs
    size = green_ref.shape[-1]
    slab, position = lax.axis_index("slab"), lax.axis_index("energy")
    energy = -4.0 + 8.0 * position.astype(f32) / (total_energies - 1)
    damping = damping_ref[0]
    for d in range(count):
        slab_ref[((slab ^ d) - slab) & (count - 1)] = blocks[d][...]
    row = lax.broadcasted_iota(jnp.int32, (size, size), 0)
    lane = lax.broadcasted_iota(jnp.int32, (size, size), 1)
    identity = jnp.where(row == lane, 1.0, 0.0).astype(f32)

    def is_last(step):
        return ((slab + step) & (count - 1)) == count - 1

    def link_of(step):
        return slab_ref[step, size // 2 + TILE :, :]

    def cut_link(step):
        return link_of(step) * jnp.where(is_last(step), 0.0, 1.0)

    def place(steps):
        for step in steps:
            diagonal_ref[step, 0] = energy * identity - unpacked(
                slab_ref[step, : size // 2, :], slab_ref[step, size // 2 : size // 2 + 1, :]
            )
            diagonal_ref[step, 1] = damping * identity

            @pl.when(is_last(step))
            def _():
                link = link_of(step)
                diagonal_ref[step, 1] = diagonal_ref[step, 1] + 0.5 * exact_dot(link, link, ((1,), (1,)))

    def subtract(node, real, imag):
        diagonal_ref[node, 0] = diagonal_ref[node, 0] - real
        diagonal_ref[node, 1] = diagonal_ref[node, 1] - imag

    place(range(1, count, 2))
    for level in range(count.bit_length() - 1):
        stride = 1 << level
        nodes = list(range(0, count, stride))
        odds = nodes[1::2]
        for first in range(0, len(odds), 2):
            group = odds[first : first + 2]
            for m, node in enumerate(group):
                work_ref[m] = diagonal_ref[node]
            invert_in_place(work_ref, len(group), count <= 4)
            if level == 0 and first == 0:
                place(range(0, count, 2))
            for m, node in enumerate(group):
                before, after = node - stride, (node + stride) % count
                middle = (work_ref[m, 0], work_ref[m, 1])
                if level == 0:
                    ends = [(cut_link(before),), (cut_link(node).T,)]
                else:
                    ends = [(link_ref[before, 0], link_ref[before, 1]), (link_ref[node, 0].T, link_ref[node, 1].T)]
                if before == after:
                    ends = [tuple(a + b for a, b in zip(*ends))]
                ends = tuple(jnp.concatenate(parts, 0) for parts in zip(*ends))
                height = ends[0].shape[0]
                if level == 0:
                    both = exact_dot(ends[0], wide(*middle), ((1,), (0,)))
                    both = jnp.concatenate([both[:, :size], both[:, size:]], 0)
                    both = exact_dot(both, ends[0], ((1,), (1,)))
                    real, imag = both[:height], both[height:]
                else:
                    both = exact_dot(wide(*ends), square(*middle), ((1,), (0,)))
                    turned = jnp.concatenate([wide(ends[0], -ends[1]), wide(ends[1], ends[0])], 0)
                    both = exact_dot(both, turned, ((1,), (1,)))
                    real, imag = both[:, :height], both[:, height:]
                subtract(before, -real[:size, :size], -imag[:size, :size])
                if before != after:
                    subtract(after, -real[size:, size:], -imag[size:, size:])
                    link_ref[before, 0] = real[:size, size:]
                    link_ref[before, 1] = imag[:size, size:]
    work_ref[0] = diagonal_ref[0]
    invert_in_place(work_ref, 1, count <= 4)
    extras = []
    for part in range(2):
        value = -work_ref[0, part]
        green_ref[part] = value
        packed_ref[part * size // 2 : (part + 1) * size // 2, :], extra = packed_half(value)
        extras.append(extra)
    which = lax.broadcasted_iota(jnp.int32, (TILE, size), 0)
    packed_ref[size:, :] = jnp.where(which == 0, extras[0], extras[1])


def green_of(blocks, damping, total_energies):
    count, size = len(blocks), blocks[0].shape[-1]
    whole = pl.BlockSpec(memory_space=pltpu.VMEM)
    scalar = pl.BlockSpec(memory_space=pltpu.SMEM)
    return pl.pallas_call(
        functools.partial(chain_kernel, count, total_energies),
        out_shape=(
            jax.ShapeDtypeStruct((2, size, size), f32),
            jax.ShapeDtypeStruct((size + TILE, size), f32),
        ),
        in_specs=[scalar] + [whole] * count,
        out_specs=(whole, whole),
        scratch_shapes=[
            pltpu.VMEM((count,) + blocks[0].shape, f32),
            pltpu.VMEM((count, 2, size, size), f32),
            pltpu.VMEM((count, 2, size, size), f32),
            pltpu.VMEM((2, 2, size, size), f32),
        ],
        compiler_params=pltpu.CompilerParams(vmem_limit_bytes=GRANT),
        name="chain",
    )(damping, *blocks)


def polar_kernel(steps, green_ref, *refs):
    groups = len(steps)
    blocks, (green_out_ref, out_ref, held, result, left) = refs[:groups], refs[groups:]
    me = lax.axis_index("energy")
    leaving = [pltpu.make_async_copy(green_ref, green_out_ref, left.at[2])]
    leaving[0].start()
    for step, block in zip(steps, blocks):
        held[me ^ step] = block[...]
    size = held.shape[-1]
    half = size // 2
    real = imag = jnp.zeros((half, size), f32)
    extra_real = extra_imag = jnp.zeros((TILE, size), f32)
    for first in range(groups):
        inside = first + me < groups
        second = jnp.where(inside, first + me, 0)
        weight = jnp.where(inside, 1.0 / groups, 0.0)
        br, bi = held[first, :half, :] * weight, held[first, half:size, :] * weight
        ar, ai = held[second, :half, :], held[second, half:size, :]
        real = real + (ar * br + ai * bi)
        imag = imag + (ai * br - ar * bi)
        b, a = held[first, size:, :] * weight, held[second, size:, :]
        br, bi, ar, ai = row_of(b, 0), row_of(b, 1), row_of(a, 0), row_of(a, 1)
        extra_real = extra_real + (ar * br + ai * bi)
        extra_imag = extra_imag + (ai * br - ar * bi)
    for part, (value, extra) in enumerate(((real, extra_real), (imag, extra_imag))):
        result[part] = unpacked(value, extra[:1])
        leaving.append(pltpu.make_async_copy(result.at[part], out_ref.at[part], left.at[part]))
        leaving[-1].start()
    for copy in leaving:
        copy.wait()


def correlate(green, packed, groups):
    def swapped(block, step):
        return lax.ppermute(block, "energy", [(s, s ^ step) for s in range(groups)])

    gathered = [(step, swapped(packed, step)) for step in range(groups - 2, 0, -2)]
    gathered.insert(0, (0, packed))
    gathered = gathered + [(step ^ 1, swapped(block, 1)) for step, block in gathered]
    steps, blocks = zip(*gathered)
    anywhere = pl.BlockSpec(memory_space=pl.ANY)
    result = jax.ShapeDtypeStruct(green.shape, f32)
    return pl.pallas_call(
        functools.partial(polar_kernel, steps),
        out_shape=(result, result),
        in_specs=[anywhere] + [pl.BlockSpec(memory_space=pltpu.VMEM)] * groups,
        out_specs=(anywhere, anywhere),
        scratch_shapes=[
            pltpu.VMEM((groups,) + packed.shape, f32),
            pltpu.VMEM(green.shape, f32),
            pltpu.SemaphoreType.DMA((3,)),
        ],
        compiler_params=pltpu.CompilerParams(vmem_limit_bytes=GRANT),
        name="polar",
    )(green, *blocks)


def correlate_spread(own, groups):
    _, size, _ = own.shape
    spread = own.reshape(2, groups, size * size // groups)
    mixed = lax.all_to_all(spread[None], "energy", split_axis=2, concat_axis=0, tiled=True)[:, :, 0]
    real, imag = mixed[:, 0], mixed[:, 1]
    pieces = []
    for offset in range(groups):
        ar, ai = real[offset:], imag[offset:]
        br, bi = real[: groups - offset], imag[: groups - offset]
        pieces.append(jnp.stack([jnp.sum(ar * br + ai * bi, 0), jnp.sum(ai * br - ar * bi, 0)]))
    result = (jnp.stack(pieces) / groups)[:, :, None, :]
    back = lax.all_to_all(result, "energy", split_axis=0, concat_axis=2, tiled=True)
    return back.reshape(own.shape)


def on_device(h_diag, coupling, broadening):
    slabs = lax.axis_size("slab")
    groups = lax.axis_size("energy")
    size = h_diag.shape[-1]
    own = jnp.concatenate([*packed_half(h_diag[0]), coupling[0]], 0)
    blocks = {0: own}
    for d in list(range(slabs - 1, 0, -2)) + list(range(slabs - 2, 0, -2)):
        blocks[d] = lax.ppermute(own, "slab", [(s, s ^ d) for s in range(slabs)])
    blocks = [blocks[d] for d in range(slabs)]
    green, packed = green_of(blocks, broadening, groups)
    if groups <= 8:
        green, polar = correlate(green, packed, groups)
    else:
        polar = correlate_spread(green, groups)
    shape = (1, 1, 2, size, size)
    return green.reshape(shape), polar.reshape(shape)


def solution(mesh):
    return jax.shard_map(
        on_device,
        mesh=mesh,
        in_specs=(P("slab", None, None), P("slab", None, None), P("energy")),
        out_specs=(P("energy", "slab", None, None, None), P("energy", "slab", None, None, None)),
        check_vma=False,
    )
```

```python
import functools

import jax
import jax.numpy as jnp
from jax import lax
from jax.experimental import pallas as pl
from jax.experimental.pallas import tpu as pltpu
from jax.sharding import PartitionSpec as P

f32 = jnp.float32
bf16 = jnp.bfloat16
PANEL = 32
TILE = 8
GRANT = 24 << 20


def three_parts(value):
    high = value.astype(bf16)
    rest = value - high.astype(f32)
    middle = rest.astype(bf16)
    low = (rest - middle.astype(f32)).astype(bf16)
    return high, middle, low


def row_of(tile, k):
    return jnp.broadcast_to(tile[k : k + 1, :], tile.shape)


def column_of(tile, k):
    return jnp.broadcast_to(tile[:, k : k + 1], tile.shape)


def lanes_at(tile, index):
    return jnp.take_along_axis(tile, index, axis=1, mode="promise_in_bounds")


def spread_columns(real, imag, base):
    index = [jnp.zeros(real.shape, jnp.int32) + (base + k) for k in range(TILE)]
    return [lanes_at(real, i) for i in index], [lanes_at(imag, i) for i in index]


def eliminate_tiles(pairs, base, row, lane):
    columns = [spread_columns(real, imag, base) for real, imag in pairs]
    pairs = list(pairs)
    for k in range(TILE):
        at_row = row == k
        at_lane = lane == base + k
        cleared = at_row | at_lane
        factors = []
        for dr, di in columns:
            pr, pi = row_of(dr[k], k), row_of(di[k], k)
            inverse = 1.0 / (pr * pr + pi * pi)
            cr, ci = jnp.where(at_row, -1.0, dr[k]), jnp.where(at_row, 0.0, di[k])
            tr, ti = cr * pr + ci * pi, ci * pr - cr * pi
            factors.append((tr, ti, inverse, tr * inverse, ti * inverse))
        for c in range(k + 1, TILE):
            for (dr, di), (tr, ti, inverse, fr, fi) in zip(columns, factors):
                ar, ai = row_of(dr[c], k), row_of(di[c], k)
                zr, zi = jnp.where(at_row, 0.0, dr[c]), jnp.where(at_row, 0.0, di[c])
                if c == k + 1:
                    dr[c] = zr - (tr * ar - ti * ai) * inverse
                    di[c] = zi - (tr * ai + ti * ar) * inverse
                else:
                    dr[c], di[c] = zr - (fr * ar - fi * ai), zi - (fr * ai + fi * ar)
        for m, ((real, imag), (_, _, _, fr, fi)) in enumerate(zip(pairs, factors)):
            ar = jnp.where(at_lane, 1.0, row_of(real, k))
            ai = jnp.where(at_lane, 0.0, row_of(imag, k))
            pairs[m] = (
                jnp.where(cleared, 0.0, real) - (fr * ar - fi * ai),
                jnp.where(cleared, 0.0, imag) - (fr * ai + fi * ar),
            )
    return pairs


def times(left, right):
    return left[0] * right[0] - left[1] * right[1], left[0] * right[1] + left[1] * right[0]


def minus(left, right):
    return left[0] - right[0], left[1] - right[1]


def eliminate_tiles_by_pairs(pairs, base, row, lane):
    columns = [spread_columns(real, imag, base) for real, imag in pairs]
    pairs = list(pairs)
    for k in range(0, TILE, 2):
        first, second = row == k, row == k + 1
        both_rows = first | second
        first_lane, second_lane = lane == base + k, lane == base + k + 1
        both_lanes = first_lane | second_lane
        cleared = both_rows | both_lanes
        ones = (jnp.where(first_lane, 1.0, 0.0), jnp.where(second_lane, 1.0, 0.0))
        factors = []
        for dr, di in columns:
            p00, p10 = [(row_of(dr[k], r), row_of(di[k], r)) for r in (k, k + 1)]
            p01, p11 = [(row_of(dr[k + 1], r), row_of(di[k + 1], r)) for r in (k, k + 1)]
            det = minus(times(p00, p11), times(p01, p10))
            inverse = 1.0 / (det[0] * det[0] + det[1] * det[1])
            conjugate = (det[0], -det[1])
            c0, c1 = [
                (
                    jnp.where(both_rows, jnp.where(own, -1.0, 0.0), dr[k + i]),
                    jnp.where(both_rows, 0.0, di[k + i]),
                )
                for i, own in enumerate((first, second))
            ]
            t0 = times(minus(times(c0, p11), times(c1, p10)), conjugate)
            t1 = times(minus(times(c1, p00), times(c0, p01)), conjugate)
            scaled = [(t[0] * inverse, t[1] * inverse) for t in (t0, t1)]
            factors.append((t0, t1, inverse, *scaled))

        def change(f0, f1, a0, a1):
            w0, w1 = times(f0, a0), times(f1, a1)
            return w0[0] + w1[0], w0[1] + w1[1]

        for c in range(k + 2, TILE):
            for (dr, di), (t0, t1, inverse, f0, f1) in zip(columns, factors):
                a0, a1 = [(row_of(dr[c], r), row_of(di[c], r)) for r in (k, k + 1)]
                zr, zi = jnp.where(both_rows, 0.0, dr[c]), jnp.where(both_rows, 0.0, di[c])
                if c < k + 4:
                    w = change(t0, t1, a0, a1)
                    dr[c], di[c] = zr - w[0] * inverse, zi - w[1] * inverse
                else:
                    w = change(f0, f1, a0, a1)
                    dr[c], di[c] = zr - w[0], zi - w[1]
        for m, ((real, imag), (_, _, _, f0, f1)) in enumerate(zip(pairs, factors)):
            a0, a1 = [
                (jnp.where(both_lanes, one, row_of(real, r)), jnp.where(both_lanes, 0.0, row_of(imag, r)))
                for one, r in zip(ones, (k, k + 1))
            ]
            w = change(f0, f1, a0, a1)
            pairs[m] = (jnp.where(cleared, 0.0, real) - w[0], jnp.where(cleared, 0.0, imag) - w[1])
    return pairs


def eliminate_panel(panels, first, row, lane):
    tiles = len(panels[0])
    for s in range(tiles):
        base = first + s * TILE
        others = [(s + 1 + u) % tiles for u in range(tiles - 1)]
        columns = [{t: spread_columns(*panel[t], base) for t in others} for panel in panels]
        eliminate = eliminate_tiles_by_pairs if len(panels) == 1 else eliminate_tiles
        done = eliminate([panel[s] for panel in panels], base, row, lane)
        rows = [[(row_of(real, k), row_of(imag, k)) for k in range(TILE)] for real, imag in done]
        inside = (lane >= base) & (lane < base + TILE)
        for t in others:
            for m, panel in enumerate(panels):
                real, imag = panel[t]
                real, imag = jnp.where(inside, 0.0, real), jnp.where(inside, 0.0, imag)
                for cr, ci, (wr, wi) in zip(*columns[m][t], rows[m]):
                    real, imag = real - (cr * wr - ci * wi), imag - (cr * wi + ci * wr)
                panel[t] = (real, imag)
        for m, panel in enumerate(panels):
            panel[s] = done[m]
    return panels


def invert_in_place(ref, count, unrolled):
    size = ref.shape[-1]
    width = min(PANEL // count, size)
    tiles = width // TILE

    def step(j, carry):
        first = j * width
        row = lax.broadcasted_iota(jnp.int32, (TILE, size), 0)
        lane = lax.broadcasted_iota(jnp.int32, (TILE, size), 1)
        panels, lefts, results = [], [], []
        for m in range(count):
            at = [pl.ds(pl.multiple_of(first + t * TILE, TILE), TILE) for t in range(tiles)]
            panels.append([(ref[m, 0, rows, :], ref[m, 1, rows, :]) for rows in at])
            parts = [real for real, _ in panels[m]] + [imag for _, imag in panels[m]]
            lh, lm, ll = three_parts(jnp.concatenate(parts, 0))
            lefts.append(jnp.concatenate([lh, lh, lm, lh, lm, ll], 0))
        panels = eliminate_panel(panels, first, row, lane)
        block = (lane >= first) & (lane < first + width)
        full_lane = lax.broadcasted_iota(jnp.int32, (size, size), 1)
        cleared = (full_lane >= first) & (full_lane < first + width)
        for m in range(count):
            wr = jnp.concatenate([jnp.where(block, -real, real) for real, _ in panels[m]], 0)
            wi = jnp.concatenate([jnp.where(block, -imag, imag) for _, imag in panels[m]], 0)
            rh, rm, rl = [square(*parts) for parts in zip(three_parts(wr), three_parts(wi))]
            change = lax.dot_general(
                lefts[m],
                jnp.concatenate([rh, rm, rh, rl, rm, rh], 0),
                (((0,), (0,)), ((), ())),
                preferred_element_type=f32,
            )
            real = jnp.where(cleared, 0.0, ref[m, 0]) - change[:, :size]
            imag = jnp.where(cleared, 0.0, ref[m, 1]) - change[:, size:]
            results.append((real, imag, wr, wi))
        for m, (real, imag, wr, wi) in enumerate(results):
            rows = pl.ds(pl.multiple_of(first, width), width)
            ref[m, 0] = real
            ref[m, 1] = imag
            ref[m, 0, rows, :] = wr
            ref[m, 1, rows, :] = wi
        return carry

    lax.fori_loop(0, size // width, step, 0, unroll=size // width if unrolled else 1)


def wide(real, imag):
    return jnp.concatenate([real, imag], 1)


def square(real, imag):
    return jnp.concatenate([wide(real, imag), wide(-imag, real)], 0)


def turned_square(real, imag):
    return jnp.concatenate([wide(real, -imag), wide(imag, real)], 0)


def half_masks(rows, size):
    row = lax.broadcasted_iota(jnp.int32, (rows, size), 0)
    lane = lax.broadcasted_iota(jnp.int32, (rows, size), 1)
    past = lax.rem(lane - row + size, size)
    return past < size // 2, (past == size // 2) & (row < size // 2)


def packed_half(value):
    size = value.shape[0]
    half = size // 2
    kept, middle = half_masks(half, size)
    upper = value[:half]
    extra = jnp.sum(jnp.where(middle, upper, 0.0), axis=0, keepdims=True)
    return jnp.where(kept, upper, value[half:]), jnp.broadcast_to(extra, (TILE, size))


def unpacked(packed, extra):
    size = packed.shape[1]
    kept, middle = half_masks(size, size)
    whole = jnp.concatenate([packed, packed], 0)
    whole = jnp.where(middle, jnp.broadcast_to(extra, (size, size)), whole)
    return jnp.where(kept | middle, whole, whole.T)


def exact_dot(left, right, dims):
    (over_left,), (over_right,) = dims
    lh, lm, ll = three_parts(left)
    if isinstance(right, tuple):
        layout, real, imag = right
        rh, rm, rl = [layout(*parts) for parts in zip(three_parts(real), three_parts(imag))]
    else:
        rh, rm, rl = three_parts(right)
    return lax.dot_general(
        jnp.concatenate([lh, lh, lm, lh, lm, ll], over_left),
        jnp.concatenate([rh, rm, rh, rl, rm, rh], over_right),
        (dims, ((), ())),
        preferred_element_type=f32,
    )


def chain_kernel(count, total_energies, damping_ref, *refs):
    blocks, refs = refs[:count], refs[count:]
    green_ref, packed_ref, slab_ref, diagonal_ref, link_ref, work_ref = refs
    size = green_ref.shape[-1]
    slab, position = lax.axis_index("slab"), lax.axis_index("energy")
    energy = -4.0 + 8.0 * position.astype(f32) / (total_energies - 1)
    damping = damping_ref[0]
    for d in range(count):
        slab_ref[((slab ^ d) - slab) & (count - 1)] = blocks[d][...]
    row = lax.broadcasted_iota(jnp.int32, (size, size), 0)
    lane = lax.broadcasted_iota(jnp.int32, (size, size), 1)
    identity = jnp.where(row == lane, 1.0, 0.0).astype(f32)

    def is_last(step):
        return ((slab + step) & (count - 1)) == count - 1

    def link_of(step):
        return slab_ref[step, size // 2 + TILE :, :]

    def cut_link(step):
        return link_of(step) * jnp.where(is_last(step), 0.0, 1.0)

    def place(steps):
        for step in steps:
            diagonal_ref[step, 0] = energy * identity - unpacked(
                slab_ref[step, : size // 2, :], slab_ref[step, size // 2 : size // 2 + 1, :]
            )
            diagonal_ref[step, 1] = damping * identity

            @pl.when(is_last(step))
            def _():
                link = link_of(step)
                diagonal_ref[step, 1] = diagonal_ref[step, 1] + 0.5 * exact_dot(link, link, ((1,), (1,)))

    def subtract(node, real, imag):
        diagonal_ref[node, 0] = diagonal_ref[node, 0] - real
        diagonal_ref[node, 1] = diagonal_ref[node, 1] - imag

    place(range(1, count, 2))
    for level in range(count.bit_length() - 1):
        stride = 1 << level
        nodes = list(range(0, count, stride))
        odds = nodes[1::2]
        for first in range(0, len(odds), 2):
            group = odds[first : first + 2]
            for m, node in enumerate(group):
                work_ref[m] = diagonal_ref[node]
            invert_in_place(work_ref, len(group), count <= 4)
            if level == 0 and first == 0:
                place(range(0, count, 2))
            for m, node in enumerate(group):
                before, after = node - stride, (node + stride) % count
                middle = (work_ref[m, 0], work_ref[m, 1])
                if level == 0:
                    ends = [(cut_link(before),), (cut_link(node).T,)]
                else:
                    ends = [(link_ref[before, 0], link_ref[before, 1]), (link_ref[node, 0].T, link_ref[node, 1].T)]
                if before == after:
                    ends = [tuple(a + b for a, b in zip(*ends))]
                ends = tuple(jnp.concatenate(parts, 0) for parts in zip(*ends))
                height = ends[0].shape[0]
                if level == 0:
                    both = exact_dot(ends[0], wide(*middle), ((1,), (0,)))
                    both = jnp.concatenate([both[:, :size], both[:, size:]], 0)
                    both = exact_dot(both, ends[0], ((1,), (1,)))
                    real, imag = both[:height], both[height:]
                else:
                    both = exact_dot(wide(*ends), (square, *middle), ((1,), (0,)))
                    both = exact_dot(both, (turned_square, *ends), ((1,), (1,)))
                    real, imag = both[:, :height], both[:, height:]
                subtract(before, -real[:size, :size], -imag[:size, :size])
                if before != after:
                    subtract(after, -real[size:, size:], -imag[size:, size:])
                    link_ref[before, 0] = real[:size, size:]
                    link_ref[before, 1] = imag[:size, size:]
    work_ref[0] = diagonal_ref[0]
    invert_in_place(work_ref, 1, count <= 4)
    extras = []
    for part in range(2):
        value = -work_ref[0, part]
        green_ref[part] = value
        packed_ref[part * size // 2 : (part + 1) * size // 2, :], extra = packed_half(value)
        extras.append(extra)
    which = lax.broadcasted_iota(jnp.int32, (TILE, size), 0)
    packed_ref[size:, :] = jnp.where(which == 0, extras[0], extras[1])


def green_of(blocks, damping, total_energies):
    count, size = len(blocks), blocks[0].shape[-1]
    whole = pl.BlockSpec(memory_space=pltpu.VMEM)
    scalar = pl.BlockSpec(memory_space=pltpu.SMEM)
    return pl.pallas_call(
        functools.partial(chain_kernel, count, total_energies),
        out_shape=(
            jax.ShapeDtypeStruct((2, size, size), f32),
            jax.ShapeDtypeStruct((size + TILE, size), f32),
        ),
        in_specs=[scalar] + [whole] * count,
        out_specs=(whole, whole),
        scratch_shapes=[
            pltpu.VMEM((count,) + blocks[0].shape, f32),
            pltpu.VMEM((count, 2, size, size), f32),
            pltpu.VMEM((count, 2, size, size), f32),
            pltpu.VMEM((2, 2, size, size), f32),
        ],
        compiler_params=pltpu.CompilerParams(vmem_limit_bytes=GRANT),
        name="chain",
    )(damping, *blocks)


def polar_kernel(steps, green_ref, *refs):
    groups = len(steps)
    blocks, (green_out_ref, out_ref, held, result, left) = refs[:groups], refs[groups:]
    me = lax.axis_index("energy")
    leaving = [pltpu.make_async_copy(green_ref, green_out_ref, left.at[2])]
    leaving[0].start()
    for step, block in zip(steps, blocks):
        held[me ^ step] = block[...]
    size = held.shape[-1]
    half = size // 2
    real = imag = jnp.zeros((half, size), f32)
    extra_real = extra_imag = jnp.zeros((TILE, size), f32)
    for first in range(groups):
        inside = first + me < groups
        second = jnp.where(inside, first + me, 0)
        weight = jnp.where(inside, 1.0 / groups, 0.0)
        br, bi = held[first, :half, :] * weight, held[first, half:size, :] * weight
        ar, ai = held[second, :half, :], held[second, half:size, :]
        real = real + (ar * br + ai * bi)
        imag = imag + (ai * br - ar * bi)
        b, a = held[first, size:, :] * weight, held[second, size:, :]
        br, bi, ar, ai = row_of(b, 0), row_of(b, 1), row_of(a, 0), row_of(a, 1)
        extra_real = extra_real + (ar * br + ai * bi)
        extra_imag = extra_imag + (ai * br - ar * bi)
    for part, (value, extra) in enumerate(((real, extra_real), (imag, extra_imag))):
        result[part] = unpacked(value, extra[:1])
        leaving.append(pltpu.make_async_copy(result.at[part], out_ref.at[part], left.at[part]))
        leaving[-1].start()
    for copy in leaving:
        copy.wait()


def correlate(green, packed, groups):
    def swapped(block, step):
        return lax.ppermute(block, "energy", [(s, s ^ step) for s in range(groups)])

    gathered = [(step, swapped(packed, step)) for step in range(groups - 2, 0, -2)]
    gathered.insert(0, (0, packed))
    gathered = gathered + [(step ^ 1, swapped(block, 1)) for step, block in gathered]
    steps, blocks = zip(*gathered)
    anywhere = pl.BlockSpec(memory_space=pl.ANY)
    result = jax.ShapeDtypeStruct(green.shape, f32)
    return pl.pallas_call(
        functools.partial(polar_kernel, steps),
        out_shape=(result, result),
        in_specs=[anywhere] + [pl.BlockSpec(memory_space=pltpu.VMEM)] * groups,
        out_specs=(anywhere, anywhere),
        scratch_shapes=[
            pltpu.VMEM((groups,) + packed.shape, f32),
            pltpu.VMEM(green.shape, f32),
            pltpu.SemaphoreType.DMA((3,)),
        ],
        compiler_params=pltpu.CompilerParams(vmem_limit_bytes=GRANT),
        name="polar",
    )(green, *blocks)


def correlate_spread(own, groups):
    _, size, _ = own.shape
    spread = own.reshape(2, groups, size * size // groups)
    mixed = lax.all_to_all(spread[None], "energy", split_axis=2, concat_axis=0, tiled=True)[:, :, 0]
    real, imag = mixed[:, 0], mixed[:, 1]
    pieces = []
    for offset in range(groups):
        ar, ai = real[offset:], imag[offset:]
        br, bi = real[: groups - offset], imag[: groups - offset]
        pieces.append(jnp.stack([jnp.sum(ar * br + ai * bi, 0), jnp.sum(ai * br - ar * bi, 0)]))
    result = (jnp.stack(pieces) / groups)[:, :, None, :]
    back = lax.all_to_all(result, "energy", split_axis=0, concat_axis=2, tiled=True)
    return back.reshape(own.shape)


def on_device(h_diag, coupling, broadening):
    slabs = lax.axis_size("slab")
    groups = lax.axis_size("energy")
    size = h_diag.shape[-1]
    own = jnp.concatenate([*packed_half(h_diag[0]), coupling[0]], 0)
    blocks = {0: own}
    for d in list(range(slabs - 1, 0, -2)) + list(range(slabs - 2, 0, -2)):
        blocks[d] = lax.ppermute(own, "slab", [(s, s ^ d) for s in range(slabs)])
    blocks = [blocks[d] for d in range(slabs)]
    green, packed = green_of(blocks, broadening, groups)
    if groups <= 8:
        green, polar = correlate(green, packed, groups)
    else:
        polar = correlate_spread(green, groups)
    shape = (1, 1, 2, size, size)
    return green.reshape(shape), polar.reshape(shape)


def solution(mesh):
    return jax.shard_map(
        on_device,
        mesh=mesh,
        in_specs=(P("slab", None, None), P("slab", None, None), P("energy")),
        out_specs=(P("energy", "slab", None, None, None), P("energy", "slab", None, None, None)),
        check_vma=False,
    )
```
